512 devices in a mesh: seq: 32 (over x, y), req: 16 (over z, core).
Axes of the slice: x: 4, y: 8, z: 8, core: 2. Of those that a mesh axis runs over, the one named last changes fastest.
Arguments:
- x_in: bfloat16 [96, 4, 1536], P('req'), may hold values from -6 to 6
- attn_gain: float32 [1536], replicated, may hold values from 0.25 to 1.75
- moe_gain: float32 [1536], replicated, may hold values from 0.25 to 1.75
- w_qkv: bfloat16 [1536, 2560], P(None, 'seq'), may hold values from -0.15625 to 0.15625
- w_o: bfloat16 [1536, 1536], P(None, 'seq'), may hold values from -0.3125 to 0.3125
- cache_k: bfloat16 [96, 4096, 512], P('req', 'seq'), may hold values from -1024 to 1024
- cache_v: bfloat16 [96, 4096, 512], P('req', 'seq'), may hold values from -6 to 6
- page_map: int32 [96, 256], P('req', 'seq'), may hold values from 0 to 255, as said below
- lengths: int32 [96], P('req'), may hold values from 2 to 4096, as said below
- routes: int32 [96, 4, 8], P('req'), may hold values from 0 to 31, all different within a row; in each aligned block of 24 rows (0 to 23, 24 to 47, ..., all dimensions but the last counted through in order) at most 12 rows name the same one
- route_weights: float32 [96, 4, 8], P('req'), may hold values from 0.1 to 1
- w_gate_up: bfloat16 [32, 1536, 1024], P('seq', 'req'), may hold values from -0.15625 to 0.15625
- w_down: bfloat16 [32, 512, 1536], P('seq', None, 'req'), may hold values from -0.375 to 0.375
Outputs:
- layer_out: bfloat16 [96, 4, 1536], P('req', None, 'seq')
The draws below stay inside these ranges and needn't reach their ends.
Inputs may be any that keep to these rules, and one draw needn't show every extreme that they name: `lengths`: every index of req holds one request with exactly 4096 cached positions. `page_map`: each row is a permutation of the request's 256 logical pages. `routes`: A token names 8 different experts. Among the 24 tokens of one index of req no expert is named more than 12 times.
All inputs are finite; a program needn't handle non-finite values.
Results may differ from the reference program's by a relative error of at most 0.01.
Values may be sent and summed in bfloat16 or wider, within the bound.
A program may use at most 64 MiB of HBM per device.

```python
import math
import jax
import jax.numpy as jnp
import numpy as np
from jax import lax

D = 1536
HEADS = 24
KVH = 8
HD = 64
FFE = 512
EXPERTS = 32
TOP = 8
NSTEP = 4
PAGE = 16
REQ_DEV = 6
R = 96
ROWS_G = 24
NPAGES = 256
MAXLEN = 4096
ATT = 1536
KVD = 512
QKV = 2560
GROUP = 3
CAP = 12
N_REQ = 16


def page_table(key):
    keys = jax.random.split(jax.random.fold_in(key, 11), R)
    return jax.vmap(lambda single: jax.random.permutation(single, NPAGES))(keys).astype(jnp.int32)


def draw_page_map(key, part):
    return page_table(key)


def draw_lengths(key, part):
    key_one, key_two, key_three, key_pick = jax.random.split(jax.random.fold_in(key, 21), 4)
    upper = MAXLEN - 2
    first = jax.random.randint(key_one, (R,), 0, upper)
    second = jax.random.randint(key_two, (R,), 0, upper)
    third = jax.random.randint(key_three, (R,), 0, upper)
    blended = first * second // MAXLEN
    blended = blended * third // MAXLEN
    picked = jax.random.randint(key_pick, (N_REQ,), 0, REQ_DEV)
    indices = jnp.arange(R, dtype=jnp.int32)
    full_length = indices % REQ_DEV == jnp.repeat(picked, REQ_DEV)
    return jnp.where(full_length, MAXLEN, 2 + blended).astype(jnp.int32)


def draw_cache_k(key, part):
    key_base = jax.random.fold_in(jax.random.fold_in(key, 31), 0)
    values = jnp.clip(jax.random.normal(key_base, (R, MAXLEN, KVD), jnp.float32), -6.0, 6.0)
    return values.astype(jnp.bfloat16)


def shard_levels(key, extent, shards, smallest, largest):
    def one(dim, parts):
        draws = jax.random.uniform(jax.random.fold_in(jax.random.fold_in(key, 6), dim), (parts,), jnp.float32, smallest / len(shards), largest / len(shards))
        return jnp.repeat(jnp.exp(draws), extent[dim] // parts).reshape((-1,) + (1,) * (len(extent) - dim - 1))

    loudness = one(*shards[0])
    for cut in shards[1:]:
        loudness = loudness * one(*cut)
    return loudness


def shared_out(rng, own, number, rows, amount, top, reach, skew):
    sequence = jax.random.permutation(rng, amount)
    crowded, common = portions_of(amount, rows * top, reach, skew, True), portions_of(amount, rows * top, reach, skew, False)
    places = jnp.arange(amount)

    def named(tallies, rotation):
        used = int((tallies > 0).sum())
        fixed = max(1, used // 4)
        shifted = fixed + (places - fixed + rotation * (used - fixed)) % max(1, amount - fixed)
        return jnp.zeros((amount,), jnp.int32).at[sequence[jnp.where(places < fixed, places, shifted)]].set(jnp.asarray(tallies, jnp.int32))

    tallies = jnp.where(number % 4 == 0, named(crowded, number // 4), named(common, number - number // 4 - 1))
    mixed = jax.random.permutation(jax.random.fold_in(own, 3), amount)
    giver, receiver = mixed[0:amount // 2 * 2:2], mixed[1:amount // 2 * 2:2]
    room = jnp.minimum(tallies[giver] - 1, reach - tallies[receiver]) // 2
    room = jnp.where((giver == sequence[0]) | (receiver == sequence[0]) | (tallies[receiver] == 0), 0, jnp.maximum(room, 0))
    shifted = jax.random.randint(jax.random.fold_in(own, 4), (amount // 2,), 0, 1 << 20) % (room + 1)
    tallies = tallies.at[giver].add(-shifted).at[receiver].add(shifted)
    labels = jnp.searchsorted(jnp.cumsum(tallies), jnp.arange(rows * top), side="right").astype(jnp.int32)
    listing = labels.reshape(top, rows).T
    listing = listing[jax.random.permutation(jax.random.fold_in(own, 1), rows)]
    rotation = jax.random.randint(jax.random.fold_in(own, 2), (rows, 1), 0, top)
    return jnp.take_along_axis(listing, (jnp.arange(top)[None, :] + rotation) % top, axis=1)


def portions_of(count, total, most, skew, full):
    portions = [(1 << 20) // math.isqrt(rank ** skew) + 1 for rank in range(1, count + 1)]
    largest = most if full else min(most, max(-(-total // count), total * portions[0] // sum(portions)))
    least = 1 if total - largest >= count - 1 else 0
    holding, surplus = [largest] + [least] * (count - 1), total - largest - least * (count - 1)
    while surplus > 0:
        free = [i for i in range(1, count) if holding[i] < largest] or [i for i in range(1, count) if holding[i] < most]
        pool, budget = sum([portions[i] for i in free]), surplus
        for i in free:
            extra = min(most - holding[i], max(1, budget * portions[i] // pool), surplus)
            holding[i] = holding[i] + extra
            surplus = surplus - extra
    return np.array(holding)


def bell_draw(own_key, dims, deviation, most, shards=(), kind=jnp.bfloat16):
    array = deviation * jax.random.normal(own_key, dims, jnp.float32)
    if shards:
        array = array * shard_levels(own_key, dims, shards, -0.22, 0.18)
    return jnp.clip(array, -most, most).astype(kind)


def setup_inputs(seed: int = 0) -> dict:
    seeds = jax.random.split(jax.random.key(seed), 14)
    x_in = bell_draw(seeds[0], (R, NSTEP, D), 1.0, 6.0, ((0, 16),))
    attn_gain = jnp.clip(1.0 + 0.15 * jax.random.normal(seeds[1], (D,), jnp.float32), 0.25, 1.75)
    moe_gain = jnp.clip(1.0 + 0.15 * jax.random.normal(seeds[2], (D,), jnp.float32), 0.25, 1.75)
    w_qkv = bell_draw(seeds[3], (D, QKV), D ** -0.5, 0.15625, ((1, 32),))
    w_o = bell_draw(seeds[4], (ATT, D), (ATT // 4) ** -0.5, 0.3125, ((1, 32),))
    cache_k = draw_cache_k(jax.random.fold_in(seeds[13], 71), 0)
    cache_v = bell_draw(seeds[6], (R, MAXLEN, KVD), 1.0, 6.0, ((0, 16), (1, 32)))
    page_map = draw_page_map(jax.random.fold_in(seeds[13], 71), 0)
    lengths = draw_lengths(jax.random.fold_in(seeds[13], 71), 0)
    routes_keys = jax.random.split(jax.random.fold_in(seeds[9], 1), R * NSTEP // ROWS_G)
    routes_turns = jax.random.permutation(jax.random.fold_in(seeds[9], 3), R * NSTEP // ROWS_G)
    routes = jax.vmap(lambda own, number: shared_out(jax.random.fold_in(seeds[9], 2), own, number, ROWS_G, EXPERTS, TOP, CAP, 1))(routes_keys, routes_turns).reshape((R, NSTEP, TOP))
    route_weights = jnp.clip(jnp.exp(math.log(1.0) - 2.3025851 * jax.random.uniform(seeds[10], (R, NSTEP, TOP), jnp.float32) ** shard_levels(seeds[10], (R, NSTEP, TOP), ((0, 16),), -0.2, 0.2)), 0.1, 1.0)
    w_gate_up = bell_draw(seeds[11], (EXPERTS, D, 2 * FFE), D ** -0.5, 0.15625, ((0, 32), (1, 16)))
    w_down = bell_draw(seeds[12], (EXPERTS, FFE, D), (FFE // 2) ** -0.5, 0.375, ((0, 32), (2, 16)))
    return {"x_in": x_in, "attn_gain": attn_gain, "moe_gain": moe_gain, "w_qkv": w_qkv, "w_o": w_o, "cache_k": cache_k, "cache_v": cache_v, "page_map": page_map, "lengths": lengths, "routes": routes, "route_weights": route_weights, "w_gate_up": w_gate_up, "w_down": w_down}


EPS = 1e-05
NEG = -1e+30

def normalize(values, gain):
    power = lax.optimization_barrier(jnp.mean(values * values, axis=-1, keepdims=True))
    return values * lax.rsqrt(power + EPS) * gain

def rotate(values, position):
    half = values.shape[-1] // 2
    rates = jnp.exp(jnp.arange(half, dtype=jnp.float32) * (-2.0 * math.log(10000.0) / values.shape[-1]))
    angle = position[..., None, None] * rates
    cosine = jnp.cos(angle)
    sine = jnp.sin(angle)
    first_half = values[..., :half]
    second_half = values[..., half:]
    return jnp.concatenate([first_half * cosine - second_half * sine, second_half * cosine + first_half * sine], axis=-1)

def reference(x_in, attn_gain, moe_gain, w_qkv, w_o, cache_k, cache_v, page_map, lengths, routes, route_weights, w_gate_up, w_down):
    requests = x_in.shape[0]
    row_count = requests * NSTEP
    inputs = x_in.astype(jnp.float32).reshape(row_count, D)
    normed = normalize(inputs, attn_gain).astype(jnp.bfloat16)
    projected = jnp.dot(normed, w_qkv, preferred_element_type=jnp.float32)
    queries = projected[:, :ATT].reshape(requests, NSTEP, HEADS, HD)
    keys_new = projected[:, ATT:ATT + KVD].reshape(requests, NSTEP, KVH, HD)
    values_new = projected[:, ATT + KVD:].reshape(requests, NSTEP, KVH, HD).astype(jnp.bfloat16)
    position = (lengths[:, None] + jnp.arange(NSTEP, dtype=jnp.int32)[None, :]).astype(jnp.float32)
    queries = rotate(queries, position).astype(jnp.bfloat16)
    keys_new = rotate(keys_new, position).astype(jnp.bfloat16)
    offsets = jnp.arange(PAGE, dtype=jnp.int32)
    causal = jnp.arange(NSTEP, dtype=jnp.int32)[:, None] >= jnp.arange(NSTEP, dtype=jnp.int32)[None, :]
    scale = HD ** (-0.5)

    def attend(items):
        query, key_fresh, value_fresh, keys, values, pages, length = items
        query = query.astype(jnp.float32).reshape(NSTEP, KVH, GROUP, HD)
        keys = keys.astype(jnp.float32).reshape(MAXLEN, KVH, HD)
        values = values.astype(jnp.float32).reshape(MAXLEN, KVH, HD)
        slot_position = (pages[:, None] * PAGE + offsets[None, :]).reshape(MAXLEN)
        live = slot_position < length
        cached = jnp.einsum('skgd,tkd->skgt', query, keys) * scale
        cached = jnp.where(live[None, None, None, :], cached, NEG)
        fresh = jnp.einsum('skgd,ukd->skgu', query, key_fresh.astype(jnp.float32)) * scale
        fresh = jnp.where(causal[:, None, None, :], fresh, NEG)
        highest = jnp.maximum(lax.optimization_barrier(jnp.max(cached, axis=-1)), lax.optimization_barrier(jnp.max(fresh, axis=-1)))
        cached_exp = jnp.exp(cached - highest[..., None])
        fresh_exp = jnp.exp(fresh - highest[..., None])
        denominator = lax.optimization_barrier(jnp.sum(cached_exp, axis=-1)) + lax.optimization_barrier(jnp.sum(fresh_exp, axis=-1))
        cached_probs = lax.optimization_barrier(cached_exp.astype(jnp.bfloat16)).astype(jnp.float32)
        fresh_probs = lax.optimization_barrier(fresh_exp.astype(jnp.bfloat16)).astype(jnp.float32)
        numerator = jnp.einsum('skgt,tkd->skgd', cached_probs, values)
        numerator = numerator + jnp.einsum('skgu,ukd->skgd', fresh_probs, value_fresh.astype(jnp.float32))
        return (numerator / denominator[..., None]).reshape(NSTEP, ATT).astype(jnp.bfloat16)
    attended = lax.map(attend, (queries, keys_new, values_new, cache_k, cache_v, page_map, lengths))
    attended = attended.reshape(row_count, ATT)
    resid = inputs + jnp.dot(attended, w_o, preferred_element_type=jnp.float32)
    mixed_in = normalize(resid, moe_gain).astype(jnp.bfloat16)
    chosen = routes.reshape(row_count, TOP)
    gates = route_weights.reshape(row_count, TOP)
    expert_ids = jnp.arange(EXPERTS, dtype=jnp.int32)
    weight_table = lax.optimization_barrier(jnp.sum(jnp.where(chosen[:, :, None] == expert_ids[None, None, :], gates[:, :, None], 0.0), axis=1))

    def expert_step(carry, items):
        weight_in, weight_out, share = items
        gate_up = jnp.dot(mixed_in, weight_in, preferred_element_type=jnp.float32)
        hidden = (jax.nn.silu(gate_up[:, :FFE]) * gate_up[:, FFE:]).astype(jnp.bfloat16)
        produced = jnp.dot(hidden, weight_out, preferred_element_type=jnp.float32)
        return (carry + share[:, None] * produced, None)
    total_mix, unused = lax.scan(expert_step, jnp.zeros((row_count, D), jnp.float32), (w_gate_up, w_down, weight_table.T))
    return (resid + total_mix).astype(jnp.bfloat16).reshape(requests, NSTEP, D)
```

```python
import math

import jax
import jax.numpy as jnp
from jax import lax
from jax.sharding import PartitionSpec as P

D = 1536
HEADS = 24
KVH = 8
HD = 64
FFE = 512
TOP = 8
NSTEP = 4
PAGE = 16
ATT = 1536
KVD = 512
GROUP = 3
CAP = 12


EPS = 1e-05
NEG = -1e30


def normalize(values, gain):
    power = jnp.mean(values * values, axis=-1, keepdims=True)
    return values * lax.rsqrt(power + EPS) * gain


def rotate(values, position):
    half = values.shape[-1] // 2
    rates = jnp.exp(
        jnp.arange(half, dtype=jnp.float32) * (-2.0 * math.log(10000.0) / values.shape[-1])
    )
    angle = position[..., None, None] * rates
    cosine = jnp.cos(angle)
    sine = jnp.sin(angle)
    first_half = values[..., :half]
    second_half = values[..., half:]
    return jnp.concatenate(
        [first_half * cosine - second_half * sine, second_half * cosine + first_half * sine],
        axis=-1,
    )


def gather_columns(part, axis_name):
    count = lax.axis_size(axis_name)
    copies = jnp.broadcast_to(part[None], (count,) + part.shape)
    pieces = lax.all_to_all(copies, axis_name, split_axis=0, concat_axis=0, tiled=True)
    rows, width = part.shape
    return jnp.moveaxis(pieces, 0, 1).reshape(rows, count * width)


def sum_scatter_columns(value, axis_name):
    count = lax.axis_size(axis_name)
    rows, width = value.shape
    chunks = jnp.moveaxis(value.reshape(rows, count, width // count), 1, 0)
    pieces = lax.all_to_all(chunks, axis_name, split_axis=0, concat_axis=0, tiled=True)
    return jnp.sum(pieces, axis=0)


def local(
    x_in,
    attn_gain,
    moe_gain,
    w_qkv,
    w_o,
    cache_k,
    cache_v,
    page_map,
    lengths,
    routes,
    route_weights,
    w_gate_up,
    w_down,
):
    expert_in = lax.all_gather(w_gate_up[0], "req", axis=0, tiled=True)
    expert_out = lax.all_gather(w_down[0], "req", axis=1, tiled=True)

    seq_count = lax.axis_size("seq")
    me = lax.axis_index("seq")
    local_requests = x_in.shape[0]
    row_count = local_requests * NSTEP
    inputs = x_in.astype(jnp.float32).reshape(row_count, D)
    normed = normalize(inputs, attn_gain).astype(jnp.bfloat16)
    projected = gather_columns(
        jnp.dot(normed, w_qkv, preferred_element_type=jnp.float32), "seq"
    )
    queries = projected[:, :ATT].reshape(local_requests, NSTEP, HEADS, HD)
    keys_new = projected[:, ATT : ATT + KVD].reshape(local_requests, NSTEP, KVH, HD)
    values_new = (
        projected[:, ATT + KVD :].reshape(local_requests, NSTEP, KVH, HD).astype(jnp.bfloat16)
    )
    position = (lengths[:, None] + jnp.arange(NSTEP, dtype=jnp.int32)[None, :]).astype(jnp.float32)
    queries = (
        rotate(queries, position)
        .astype(jnp.bfloat16)
        .reshape(local_requests, NSTEP, KVH, GROUP, HD)
    )
    keys_new = rotate(keys_new, position).astype(jnp.bfloat16)
    scale = HD ** (-0.5)
    slot_count = cache_k.shape[1]
    cached_keys = cache_k.reshape(local_requests, slot_count, KVH, HD)
    cached_values = cache_v.reshape(local_requests, slot_count, KVH, HD)
    slot_position = (
        page_map[:, :, None] * PAGE + jnp.arange(PAGE, dtype=jnp.int32)[None, None, :]
    ).reshape(local_requests, slot_count)
    live = (slot_position < lengths[:, None])[:, None, None, None, :]
    scores = (
        jnp.einsum("rskgd,rtkd->rskgt", queries, cached_keys, preferred_element_type=jnp.float32)
        * scale
    )
    scores = jnp.where(live, scores, NEG)
    local_top = jnp.max(scores, axis=-1)
    exp_scores = jnp.where(live, jnp.exp(scores - local_top[..., None]), 0.0)
    local_total = jnp.sum(exp_scores, axis=-1).reshape(row_count, HEADS)
    local_sums = jnp.einsum(
        "rskgt,rtkd->rskgd",
        exp_scores.astype(jnp.bfloat16),
        cached_values,
        preferred_element_type=jnp.float32,
    ).reshape(row_count, ATT)
    local_top = local_top.reshape(row_count, HEADS)

    width = ATT // seq_count
    sum_chunks = jnp.moveaxis(local_sums.reshape(row_count, seq_count, width), 1, 0)
    extras = jnp.broadcast_to(
        jnp.concatenate([local_total, local_top], axis=1)[None],
        (seq_count, row_count, 2 * HEADS),
    )
    outgoing = jnp.concatenate([sum_chunks, extras], axis=2)
    arrived = lax.all_to_all(outgoing, "seq", split_axis=0, concat_axis=0, tiled=True)
    part_sums = arrived[:, :, :width]
    part_totals = arrived[:, :, width : width + HEADS]
    part_tops = arrived[:, :, width + HEADS :]

    causal = (
        jnp.arange(NSTEP, dtype=jnp.int32)[:, None] >= jnp.arange(NSTEP, dtype=jnp.int32)[None, :]
    )[None, :, None, None, :]
    fresh = (
        jnp.einsum("rskgd,rukd->rskgu", queries, keys_new, preferred_element_type=jnp.float32)
        * scale
    )
    fresh = jnp.where(causal, fresh, NEG).reshape(row_count, HEADS, NSTEP)
    cache_top = jnp.max(part_tops, axis=0)
    highest = jnp.maximum(cache_top, jnp.max(fresh, axis=-1))
    factors = jnp.exp(part_tops - highest[None])
    fresh_exp = jnp.exp(fresh - highest[:, :, None])
    denominator = jnp.sum(part_totals * factors, axis=0) + jnp.sum(fresh_exp, axis=-1)
    fresh_probs = fresh_exp.reshape(local_requests, NSTEP, KVH, GROUP, NSTEP).astype(jnp.bfloat16)
    fresh_sums = jnp.einsum(
        "rskgu,rukd->rskgd", fresh_probs, values_new, preferred_element_type=jnp.float32
    ).reshape(row_count, ATT)
    start = me * width
    head_of = (start + jnp.arange(width, dtype=jnp.int32)) // HD
    chunk_factors = jnp.take(factors, head_of, axis=2)
    numerator = jnp.sum(part_sums * chunk_factors, axis=0) + lax.dynamic_slice_in_dim(
        fresh_sums, start, width, 1
    )
    chunk_denominator = jnp.take(denominator, head_of, axis=1)
    attended_part = (numerator / chunk_denominator).astype(jnp.bfloat16)
    attended = gather_columns(attended_part, "seq")
    attn_mixed = gather_columns(
        jnp.dot(attended, w_o, preferred_element_type=jnp.float32), "seq"
    )
    resid = inputs + attn_mixed
    mixed_in = normalize(resid, moe_gain).astype(jnp.bfloat16)

    expert = me
    chosen = routes.reshape(row_count, TOP)
    gates = route_weights.reshape(row_count, TOP)
    route_scale = jnp.sum(jnp.where(chosen == expert, gates, 0.0), axis=-1)
    gate_up = jnp.dot(mixed_in, expert_in, preferred_element_type=jnp.float32)
    hidden = (jax.nn.silu(gate_up[:, :FFE]) * gate_up[:, FFE:]).astype(jnp.bfloat16)
    produced = jnp.dot(hidden, expert_out, preferred_element_type=jnp.float32)
    own_share = sum_scatter_columns(route_scale[:, None] * produced, "seq")
    share_width = own_share.shape[1]
    resid_share = lax.dynamic_slice_in_dim(resid, me * share_width, share_width, 1)
    return (
        (resid_share + own_share).astype(jnp.bfloat16).reshape(local_requests, NSTEP, share_width)
    )


def solution(mesh):
    in_specs = (
        P("req", None, None),
        P(),
        P(),
        P(None, "seq"),
        P(None, "seq"),
        P("req", "seq", None),
        P("req", "seq", None),
        P("req", "seq"),
        P("req"),
        P("req", None, None),
        P("req", None, None),
        P("seq", "req", None),
        P("seq", None, "req"),
    )
    out_specs = P("req", None, "seq")
    return jax.shard_map(local, mesh=mesh, in_specs=in_specs, out_specs=out_specs, check_vma=False)
```

```python
import functools
import math

import jax
import jax.numpy as jnp
from jax import lax
from jax.experimental import pallas as pl
from jax.experimental.pallas import tpu as pltpu
from jax.sharding import PartitionSpec as P

D = 1536
HEADS = 24
KVH = 8
HD = 64
FFE = 512
TOP = 8
NSTEP = 4
PAGE = 16
ATT = 1536
KVD = 512
GROUP = 3
CAP = 12


EPS = 1e-05
NEG = -1e30


def normalize(values, gain):
    power = jnp.mean(values * values, axis=-1, keepdims=True)
    return values * lax.rsqrt(power + EPS) * gain


def rotate(values, position):
    half = values.shape[-1] // 2
    rates = jnp.exp(
        jnp.arange(half, dtype=jnp.float32) * (-2.0 * math.log(10000.0) / values.shape[-1])
    )
    angle = position[..., None, None] * rates
    cosine = jnp.cos(angle)
    sine = jnp.sin(angle)
    first_half = values[..., :half]
    second_half = values[..., half:]
    return jnp.concatenate(
        [first_half * cosine - second_half * sine, second_half * cosine + first_half * sine],
        axis=-1,
    )


MESH = pl.DeviceIdType.MESH


def exchange_kernel(count, axis_name, gather, x_ref, o_ref, send_sem, recv_sem):
    me = lax.axis_index(axis_name)
    barrier = pltpu.get_barrier_semaphore()

    def greet(k, carry):
        peer = lax.rem(me + k, count)
        pl.semaphore_signal(barrier, inc=1, device_id={axis_name: peer}, device_id_type=MESH)
        return carry

    lax.fori_loop(1, count, greet, 0)
    pl.semaphore_wait(barrier, count - 1)

    def describe(k):
        peer = lax.rem(me + k, count)
        return pltpu.make_async_remote_copy(
            src_ref=x_ref if gather else x_ref.at[peer],
            dst_ref=o_ref.at[me],
            send_sem=send_sem.at[k],
            recv_sem=recv_sem.at[k],
            device_id={axis_name: peer},
            device_id_type=MESH,
        )

    def send(k, carry):
        describe(k).start()
        return carry

    lax.fori_loop(1, count, send, 0)
    o_ref[me] = x_ref[...] if gather else x_ref[me]

    def finish(k, carry):
        describe(k).wait()
        return carry

    lax.fori_loop(1, count, finish, 0)


def exchange(value, axis_name, collective_id, gather):
    count = lax.axis_size(axis_name)
    shape = value.shape if not gather else (count,) + value.shape
    return pl.pallas_call(
        functools.partial(exchange_kernel, count, axis_name, gather),
        out_shape=jax.ShapeDtypeStruct(shape, value.dtype),
        in_specs=[pl.BlockSpec(memory_space=pltpu.VMEM)],
        out_specs=pl.BlockSpec(memory_space=pltpu.VMEM),
        scratch_shapes=[
            pltpu.SemaphoreType.DMA((count,)),
            pltpu.SemaphoreType.DMA((count,)),
        ],
        compiler_params=pltpu.CompilerParams(collective_id=collective_id, has_side_effects=True),
    )(value)


def gather_columns(part, axis_name, collective_id):
    count = lax.axis_size(axis_name)
    pieces = exchange(part.astype(jnp.float32), axis_name, collective_id, True)
    rows, width = part.shape
    return jnp.moveaxis(pieces, 0, 1).reshape(rows, count * width).astype(part.dtype)


def sum_scatter_columns(value, axis_name, collective_id):
    count = lax.axis_size(axis_name)
    rows, width = value.shape
    chunks = jnp.moveaxis(value.reshape(rows, count, width // count), 1, 0)
    pieces = exchange(chunks, axis_name, collective_id, False)
    return jnp.sum(pieces, axis=0)


def local(
    x_in,
    attn_gain,
    moe_gain,
    w_qkv,
    w_o,
    cache_k,
    cache_v,
    page_map,
    lengths,
    routes,
    route_weights,
    w_gate_up,
    w_down,
):
    expert_in = lax.all_gather(w_gate_up[0], "req", axis=0, tiled=True)
    expert_out = lax.all_gather(w_down[0], "req", axis=1, tiled=True)

    seq_count = lax.axis_size("seq")
    me = lax.axis_index("seq")
    local_requests = x_in.shape[0]
    row_count = local_requests * NSTEP
    inputs = x_in.astype(jnp.float32).reshape(row_count, D)
    normed = normalize(inputs, attn_gain).astype(jnp.bfloat16)
    projected = gather_columns(
        jnp.dot(normed, w_qkv, preferred_element_type=jnp.float32), "seq", 0
    )
    queries = projected[:, :ATT].reshape(local_requests, NSTEP, HEADS, HD)
    keys_new = projected[:, ATT : ATT + KVD].reshape(local_requests, NSTEP, KVH, HD)
    values_new = (
        projected[:, ATT + KVD :].reshape(local_requests, NSTEP, KVH, HD).astype(jnp.bfloat16)
    )
    position = (lengths[:, None] + jnp.arange(NSTEP, dtype=jnp.int32)[None, :]).astype(jnp.float32)
    queries = (
        rotate(queries, position)
        .astype(jnp.bfloat16)
        .reshape(local_requests, NSTEP, KVH, GROUP, HD)
    )
    keys_new = rotate(keys_new, position).astype(jnp.bfloat16)
    scale = HD ** (-0.5)
    slot_count = cache_k.shape[1]
    cached_keys = cache_k.reshape(local_requests, slot_count, KVH, HD)
    cached_values = cache_v.reshape(local_requests, slot_count, KVH, HD)
    slot_position = (
        page_map[:, :, None] * PAGE + jnp.arange(PAGE, dtype=jnp.int32)[None, None, :]
    ).reshape(local_requests, slot_count)
    live = (slot_position < lengths[:, None])[:, None, None, None, :]
    scores = (
        jnp.einsum("rskgd,rtkd->rskgt", queries, cached_keys, preferred_element_type=jnp.float32)
        * scale
    )
    scores = jnp.where(live, scores, NEG)
    local_top = jnp.max(scores, axis=-1)
    exp_scores = jnp.where(live, jnp.exp(scores - local_top[..., None]), 0.0)
    local_total = jnp.sum(exp_scores, axis=-1).reshape(row_count, HEADS)
    local_sums = jnp.einsum(
        "rskgt,rtkd->rskgd",
        exp_scores.astype(jnp.bfloat16),
        cached_values,
        preferred_element_type=jnp.float32,
    ).reshape(row_count, ATT)
    local_top = local_top.reshape(row_count, HEADS)

    width = ATT // seq_count
    sum_chunks = jnp.moveaxis(local_sums.reshape(row_count, seq_count, width), 1, 0)
    extras = jnp.broadcast_to(
        jnp.concatenate([local_total, local_top], axis=1)[None],
        (seq_count, row_count, 2 * HEADS),
    )
    outgoing = jnp.concatenate([sum_chunks, extras], axis=2)
    arrived = exchange(outgoing, "seq", 1, False)
    part_sums = arrived[:, :, :width]
    part_totals = arrived[:, :, width : width + HEADS]
    part_tops = arrived[:, :, width + HEADS :]

    causal = (
        jnp.arange(NSTEP, dtype=jnp.int32)[:, None] >= jnp.arange(NSTEP, dtype=jnp.int32)[None, :]
    )[None, :, None, None, :]
    fresh = (
        jnp.einsum("rskgd,rukd->rskgu", queries, keys_new, preferred_element_type=jnp.float32)
        * scale
    )
    fresh = jnp.where(causal, fresh, NEG).reshape(row_count, HEADS, NSTEP)
    cache_top = jnp.max(part_tops, axis=0)
    highest = jnp.maximum(cache_top, jnp.max(fresh, axis=-1))
    factors = jnp.exp(part_tops - highest[None])
    fresh_exp = jnp.exp(fresh - highest[:, :, None])
    denominator = jnp.sum(part_totals * factors, axis=0) + jnp.sum(fresh_exp, axis=-1)
    fresh_probs = fresh_exp.reshape(local_requests, NSTEP, KVH, GROUP, NSTEP).astype(jnp.bfloat16)
    fresh_sums = jnp.einsum(
        "rskgu,rukd->rskgd", fresh_probs, values_new, preferred_element_type=jnp.float32
    ).reshape(row_count, ATT)
    start = me * width
    head_of = (start + jnp.arange(width, dtype=jnp.int32)) // HD
    chunk_factors = jnp.take(factors, head_of, axis=2)
    numerator = jnp.sum(part_sums * chunk_factors, axis=0) + lax.dynamic_slice_in_dim(
        fresh_sums, start, width, 1
    )
    chunk_denominator = jnp.take(denominator, head_of, axis=1)
    attended_part = (numerator / chunk_denominator).astype(jnp.bfloat16)
    attended = gather_columns(attended_part, "seq", 2)
    attn_mixed = gather_columns(
        jnp.dot(attended, w_o, preferred_element_type=jnp.float32), "seq", 3
    )
    resid = inputs + attn_mixed
    mixed_in = normalize(resid, moe_gain).astype(jnp.bfloat16)

    expert = me
    chosen = routes.reshape(row_count, TOP)
    gates = route_weights.reshape(row_count, TOP)
    route_scale = jnp.sum(jnp.where(chosen == expert, gates, 0.0), axis=-1)
    gate_up = jnp.dot(mixed_in, expert_in, preferred_element_type=jnp.float32)
    hidden = (jax.nn.silu(gate_up[:, :FFE]) * gate_up[:, FFE:]).astype(jnp.bfloat16)
    produced = jnp.dot(hidden, expert_out, preferred_element_type=jnp.float32)
    own_share = sum_scatter_columns(route_scale[:, None] * produced, "seq", 4)
    share_width = own_share.shape[1]
    resid_share = lax.dynamic_slice_in_dim(resid, me * share_width, share_width, 1)
    return (
        (resid_share + own_share).astype(jnp.bfloat16).reshape(local_requests, NSTEP, share_width)
    )


def solution(mesh):
    in_specs = (
        P("req", None, None),
        P(),
        P(),
        P(None, "seq"),
        P(None, "seq"),
        P("req", "seq", None),
        P("req", "seq", None),
        P("req", "seq"),
        P("req"),
        P("req", None, None),
        P("req", None, None),
        P("seq", "req", None),
        P("seq", None, "req"),
    )
    out_specs = P("req", None, "seq")
    return jax.shard_map(local, mesh=mesh, in_specs=in_specs, out_specs=out_specs, check_vma=False)
```

```python
import math

import jax
import jax.numpy as jnp
from jax import lax
from jax.sharding import PartitionSpec as P

D = 1536
HEADS = 24
KVH = 8
HD = 64
FFE = 512
TOP = 8
NSTEP = 4
PAGE = 16
ATT = 1536
KVD = 512
GROUP = 3
CAP = 12


EPS = 1e-05
NEG = -1e30


def normalize(values, gain):
    power = jnp.mean(values * values, axis=-1, keepdims=True)
    return values * lax.rsqrt(power + EPS) * gain


def rotate(values, position):
    half = values.shape[-1] // 2
    rates = jnp.exp(
        jnp.arange(half, dtype=jnp.float32) * (-2.0 * math.log(10000.0) / values.shape[-1])
    )
    angle = position[..., None, None] * rates
    cosine = jnp.cos(angle)
    sine = jnp.sin(angle)
    first_half = values[..., :half]
    second_half = values[..., half:]
    return jnp.concatenate(
        [first_half * cosine - second_half * sine, second_half * cosine + first_half * sine],
        axis=-1,
    )


def gather_columns(part, axis_name):
    count = lax.axis_size(axis_name)
    copies = jnp.broadcast_to(part[None], (count,) + part.shape)
    pieces = lax.all_to_all(copies, axis_name, split_axis=0, concat_axis=0, tiled=True)
    rows, width = part.shape
    return jnp.moveaxis(pieces, 0, 1).reshape(rows, count * width)


def sum_scatter_columns(value, axis_name):
    count = lax.axis_size(axis_name)
    rows, width = value.shape
    chunks = jnp.moveaxis(value.reshape(rows, count, width // count), 1, 0)
    pieces = lax.all_to_all(chunks, axis_name, split_axis=0, concat_axis=0, tiled=True)
    return jnp.sum(pieces, axis=0)


def local(
    x_in,
    attn_gain,
    moe_gain,
    w_qkv,
    w_o,
    cache_k,
    cache_v,
    page_map,
    lengths,
    routes,
    route_weights,
    w_gate_up,
    w_down,
):
    pieces = 4
    expert_in = jnp.concatenate(
        [
            lax.all_gather(part, "req", axis=0, tiled=True)
            for part in jnp.split(w_gate_up[0], pieces, axis=1)
        ],
        axis=1,
    )
    expert_out = jnp.concatenate(
        [
            lax.all_gather(part, "req", axis=1, tiled=True)
            for part in jnp.split(w_down[0], pieces // 2, axis=0)
        ],
        axis=0,
    )

    seq_count = lax.axis_size("seq")
    me = lax.axis_index("seq")
    local_requests = x_in.shape[0]
    row_count = local_requests * NSTEP
    inputs = x_in.astype(jnp.float32).reshape(row_count, D)
    normed = normalize(inputs, attn_gain).astype(jnp.bfloat16)
    projected = gather_columns(
        jnp.dot(normed, w_qkv, preferred_element_type=jnp.float32), "seq"
    )
    queries = projected[:, :ATT].reshape(local_requests, NSTEP, HEADS, HD)
    keys_new = projected[:, ATT : ATT + KVD].reshape(local_requests, NSTEP, KVH, HD)
    values_new = (
        projected[:, ATT + KVD :].reshape(local_requests, NSTEP, KVH, HD).astype(jnp.bfloat16)
    )
    position = (lengths[:, None] + jnp.arange(NSTEP, dtype=jnp.int32)[None, :]).astype(jnp.float32)
    queries = (
        rotate(queries, position)
        .astype(jnp.bfloat16)
        .reshape(local_requests, NSTEP, KVH, GROUP, HD)
    )
    keys_new = rotate(keys_new, position).astype(jnp.bfloat16)
    scale = HD ** (-0.5)
    slot_count = cache_k.shape[1]
    cached_keys = cache_k.reshape(local_requests, slot_count, KVH, HD)
    cached_values = cache_v.reshape(local_requests, slot_count, KVH, HD)
    slot_position = (
        page_map[:, :, None] * PAGE + jnp.arange(PAGE, dtype=jnp.int32)[None, None, :]
    ).reshape(local_requests, slot_count)
    live = (slot_position < lengths[:, None])[:, None, None, None, :]
    scores = (
        jnp.einsum("rskgd,rtkd->rskgt", queries, cached_keys, preferred_element_type=jnp.float32)
        * scale
    )
    scores = jnp.where(live, scores, NEG)
    local_top = jnp.max(scores, axis=-1)
    exp_scores = jnp.where(live, jnp.exp(scores - local_top[..., None]), 0.0)
    local_total = jnp.sum(exp_scores, axis=-1).reshape(row_count, HEADS)
    local_sums = jnp.einsum(
        "rskgt,rtkd->rskgd",
        exp_scores.astype(jnp.bfloat16),
        cached_values,
        preferred_element_type=jnp.float32,
    ).reshape(row_count, ATT)
    local_top = local_top.reshape(row_count, HEADS)

    width = ATT // seq_count
    sum_chunks = jnp.moveaxis(local_sums.reshape(row_count, seq_count, width), 1, 0)
    extras = jnp.broadcast_to(
        jnp.concatenate([local_total, local_top], axis=1)[None],
        (seq_count, row_count, 2 * HEADS),
    )
    outgoing = jnp.concatenate([sum_chunks, extras], axis=2)
    arrived = lax.all_to_all(outgoing, "seq", split_axis=0, concat_axis=0, tiled=True)
    part_sums = arrived[:, :, :width]
    part_totals = arrived[:, :, width : width + HEADS]
    part_tops = arrived[:, :, width + HEADS :]

    causal = (
        jnp.arange(NSTEP, dtype=jnp.int32)[:, None] >= jnp.arange(NSTEP, dtype=jnp.int32)[None, :]
    )[None, :, None, None, :]
    fresh = (
        jnp.einsum("rskgd,rukd->rskgu", queries, keys_new, preferred_element_type=jnp.float32)
        * scale
    )
    fresh = jnp.where(causal, fresh, NEG).reshape(row_count, HEADS, NSTEP)
    cache_top = jnp.max(part_tops, axis=0)
    highest = jnp.maximum(cache_top, jnp.max(fresh, axis=-1))
    factors = jnp.exp(part_tops - highest[None])
    fresh_exp = jnp.exp(fresh - highest[:, :, None])
    denominator = jnp.sum(part_totals * factors, axis=0) + jnp.sum(fresh_exp, axis=-1)
    fresh_probs = fresh_exp.reshape(local_requests, NSTEP, KVH, GROUP, NSTEP).astype(jnp.bfloat16)
    fresh_sums = jnp.einsum(
        "rskgu,rukd->rskgd", fresh_probs, values_new, preferred_element_type=jnp.float32
    ).reshape(row_count, ATT)
    start = me * width
    head_of = (start + jnp.arange(width, dtype=jnp.int32)) // HD
    chunk_factors = jnp.take(factors, head_of, axis=2)
    numerator = jnp.sum(part_sums * chunk_factors, axis=0) + lax.dynamic_slice_in_dim(
        fresh_sums, start, width, 1
    )
    chunk_denominator = jnp.take(denominator, head_of, axis=1)
    attended_part = (numerator / chunk_denominator).astype(jnp.bfloat16)
    attended = gather_columns(attended_part, "seq")
    attn_mixed = gather_columns(
        jnp.dot(attended, w_o, preferred_element_type=jnp.float32), "seq"
    )
    resid = inputs + attn_mixed
    mixed_in = normalize(resid, moe_gain).astype(jnp.bfloat16)

    expert = me
    chosen = routes.reshape(row_count, TOP)
    gates = route_weights.reshape(row_count, TOP)
    route_scale = jnp.sum(jnp.where(chosen == expert, gates, 0.0), axis=-1)
    gate_up = jnp.dot(mixed_in, expert_in, preferred_element_type=jnp.float32)
    hidden = (jax.nn.silu(gate_up[:, :FFE]) * gate_up[:, FFE:]).astype(jnp.bfloat16)
    produced = jnp.dot(hidden, expert_out, preferred_element_type=jnp.float32)
    own_share = sum_scatter_columns(route_scale[:, None] * produced, "seq")
    share_width = own_share.shape[1]
    resid_share = lax.dynamic_slice_in_dim(resid, me * share_width, share_width, 1)
    return (
        (resid_share + own_share).astype(jnp.bfloat16).reshape(local_requests, NSTEP, share_width)
    )


def solution(mesh):
    in_specs = (
        P("req", None, None),
        P(),
        P(),
        P(None, "seq"),
        P(None, "seq"),
        P("req", "seq", None),
        P("req", "seq", None),
        P("req", "seq"),
        P("req"),
        P("req", None, None),
        P("req", None, None),
        P("seq", "req", None),
        P("seq", None, "req"),
    )
    out_specs = P("req", None, "seq")
    return jax.shard_map(local, mesh=mesh, in_specs=in_specs, out_specs=out_specs, check_vma=False)
```

```python
import functools
import math

import jax
import jax.numpy as jnp
from jax import lax
from jax.experimental import pallas as pl
from jax.experimental.pallas import tpu as pltpu
from jax.sharding import PartitionSpec as P

D = 1536
HEADS = 24
KVH = 8
HD = 64
FFE = 512
TOP = 8
NSTEP = 4
PAGE = 16
ATT = 1536
KVD = 512
GROUP = 3
CAP = 12


EPS = 1e-05
NEG = -1e30


def normalize(values, gain):
    power = jnp.mean(values * values, axis=-1, keepdims=True)
    return values * lax.rsqrt(power + EPS) * gain


def rotate(values, position):
    half = values.shape[-1] // 2
    rates = jnp.exp(
        jnp.arange(half, dtype=jnp.float32) * (-2.0 * math.log(10000.0) / values.shape[-1])
    )
    angle = position[..., None, None] * rates
    cosine = jnp.cos(angle)
    sine = jnp.sin(angle)
    first_half = values[..., :half]
    second_half = values[..., half:]
    return jnp.concatenate(
        [first_half * cosine - second_half * sine, second_half * cosine + first_half * sine],
        axis=-1,
    )


def gather_columns(part, axis_name):
    count = lax.axis_size(axis_name)
    copies = jnp.broadcast_to(part[None], (count,) + part.shape)
    pieces = lax.all_to_all(copies, axis_name, split_axis=0, concat_axis=0, tiled=True)
    rows, width = part.shape
    return jnp.moveaxis(pieces, 0, 1).reshape(rows, count * width)


def sum_scatter_columns(value, axis_name):
    count = lax.axis_size(axis_name)
    rows, width = value.shape
    chunks = jnp.moveaxis(value.reshape(rows, count, width // count), 1, 0)
    pieces = lax.all_to_all(chunks, axis_name, split_axis=0, concat_axis=0, tiled=True)
    return jnp.sum(pieces, axis=0)


MESH = pl.DeviceIdType.MESH


def mixed_kernel(count, axis_name, part_ref, wt_ref, o_ref, full, mine, send_sem, recv_sem, own_sem):
    me = lax.axis_index(axis_name)
    width = part_ref.shape[0]
    rows = pl.ds(pl.multiple_of(me * width, 8), width)
    barrier = pltpu.get_barrier_semaphore()

    def greet(k, carry):
        peer = lax.rem(me + k, count)
        pl.semaphore_signal(barrier, inc=1, device_id={axis_name: peer}, device_id_type=MESH)
        return carry

    lax.fori_loop(1, count, greet, 0)
    pl.semaphore_wait(barrier, count - 1)

    def spread(stage, source, target):
        def describe(k):
            peer = lax.rem(me + k, count)
            return pltpu.make_async_remote_copy(
                src_ref=source,
                dst_ref=target.at[rows],
                send_sem=send_sem.at[stage, k],
                recv_sem=recv_sem.at[stage, k],
                device_id={axis_name: peer},
                device_id_type=MESH,
            )

        def send(k, carry):
            describe(k).start()
            return carry

        def finish(k, carry):
            describe(k).wait()
            return carry

        lax.fori_loop(1, count, send, 0)
        own = pltpu.make_async_copy(source, target.at[rows], own_sem.at[stage])
        own.start()
        lax.fori_loop(1, count, finish, 0)
        own.wait()

    spread(0, part_ref, full)
    mine[...] = jnp.dot(
        wt_ref[...], full[...].astype(jnp.bfloat16), preferred_element_type=jnp.float32
    )
    spread(1, mine, o_ref)


def project_out(attended_part, w_o, axis_name, collective_id):
    count = lax.axis_size(axis_name)
    rows, width = attended_part.shape
    out_t = pl.pallas_call(
        functools.partial(mixed_kernel, count, axis_name),
        out_shape=jax.ShapeDtypeStruct((count * width, rows), jnp.float32),
        in_specs=[pl.BlockSpec(memory_space=pltpu.VMEM)] * 2,
        out_specs=pl.BlockSpec(memory_space=pltpu.VMEM),
        scratch_shapes=[
            pltpu.VMEM((count * width, rows), jnp.float32),
            pltpu.VMEM((width, rows), jnp.float32),
            pltpu.SemaphoreType.DMA((2, count)),
            pltpu.SemaphoreType.DMA((2, count)),
            pltpu.SemaphoreType.DMA((2,)),
        ],
        compiler_params=pltpu.CompilerParams(collective_id=collective_id, has_side_effects=True),
    )(attended_part.astype(jnp.float32).T, w_o.T)
    return out_t.T


def local(
    x_in,
    attn_gain,
    moe_gain,
    w_qkv,
    w_o,
    cache_k,
    cache_v,
    page_map,
    lengths,
    routes,
    route_weights,
    w_gate_up,
    w_down,
):
    expert_in = lax.all_gather(w_gate_up[0], "req", axis=0, tiled=True)
    expert_out = lax.all_gather(w_down[0], "req", axis=1, tiled=True)

    seq_count = lax.axis_size("seq")
    me = lax.axis_index("seq")
    local_requests = x_in.shape[0]
    row_count = local_requests * NSTEP
    inputs = x_in.astype(jnp.float32).reshape(row_count, D)
    normed = normalize(inputs, attn_gain).astype(jnp.bfloat16)
    projected = gather_columns(
        jnp.dot(normed, w_qkv, preferred_element_type=jnp.float32), "seq"
    )
    queries = projected[:, :ATT].reshape(local_requests, NSTEP, HEADS, HD)
    keys_new = projected[:, ATT : ATT + KVD].reshape(local_requests, NSTEP, KVH, HD)
    values_new = (
        projected[:, ATT + KVD :].reshape(local_requests, NSTEP, KVH, HD).astype(jnp.bfloat16)
    )
    position = (lengths[:, None] + jnp.arange(NSTEP, dtype=jnp.int32)[None, :]).astype(jnp.float32)
    queries = (
        rotate(queries, position)
        .astype(jnp.bfloat16)
        .reshape(local_requests, NSTEP, KVH, GROUP, HD)
    )
    keys_new = rotate(keys_new, position).astype(jnp.bfloat16)
    scale = HD ** (-0.5)
    slot_count = cache_k.shape[1]
    cached_keys = cache_k.reshape(local_requests, slot_count, KVH, HD)
    cached_values = cache_v.reshape(local_requests, slot_count, KVH, HD)
    slot_position = (
        page_map[:, :, None] * PAGE + jnp.arange(PAGE, dtype=jnp.int32)[None, None, :]
    ).reshape(local_requests, slot_count)
    live = (slot_position < lengths[:, None])[:, None, None, None, :]
    scores = (
        jnp.einsum("rskgd,rtkd->rskgt", queries, cached_keys, preferred_element_type=jnp.float32)
        * scale
    )
    scores = jnp.where(live, scores, NEG)
    local_top = jnp.max(scores, axis=-1)
    exp_scores = jnp.where(live, jnp.exp(scores - local_top[..., None]), 0.0)
    local_total = jnp.sum(exp_scores, axis=-1).reshape(row_count, HEADS)
    local_sums = jnp.einsum(
        "rskgt,rtkd->rskgd",
        exp_scores.astype(jnp.bfloat16),
        cached_values,
        preferred_element_type=jnp.float32,
    ).reshape(row_count, ATT)
    local_top = local_top.reshape(row_count, HEADS)

    width = ATT // seq_count
    sum_chunks = jnp.moveaxis(local_sums.reshape(row_count, seq_count, width), 1, 0)
    extras = jnp.broadcast_to(
        jnp.concatenate([local_total, local_top], axis=1)[None],
        (seq_count, row_count, 2 * HEADS),
    )
    outgoing = jnp.concatenate([sum_chunks, extras], axis=2)
    arrived = lax.all_to_all(outgoing, "seq", split_axis=0, concat_axis=0, tiled=True)
    part_sums = arrived[:, :, :width]
    part_totals = arrived[:, :, width : width + HEADS]
    part_tops = arrived[:, :, width + HEADS :]

    causal = (
        jnp.arange(NSTEP, dtype=jnp.int32)[:, None] >= jnp.arange(NSTEP, dtype=jnp.int32)[None, :]
    )[None, :, None, None, :]
    fresh = (
        jnp.einsum("rskgd,rukd->rskgu", queries, keys_new, preferred_element_type=jnp.float32)
        * scale
    )
    fresh = jnp.where(causal, fresh, NEG).reshape(row_count, HEADS, NSTEP)
    cache_top = jnp.max(part_tops, axis=0)
    highest = jnp.maximum(cache_top, jnp.max(fresh, axis=-1))
    factors = jnp.exp(part_tops - highest[None])
    fresh_exp = jnp.exp(fresh - highest[:, :, None])
    denominator = jnp.sum(part_totals * factors, axis=0) + jnp.sum(fresh_exp, axis=-1)
    fresh_probs = fresh_exp.reshape(local_requests, NSTEP, KVH, GROUP, NSTEP).astype(jnp.bfloat16)
    fresh_sums = jnp.einsum(
        "rskgu,rukd->rskgd", fresh_probs, values_new, preferred_element_type=jnp.float32
    ).reshape(row_count, ATT)
    start = me * width
    head_of = (start + jnp.arange(width, dtype=jnp.int32)) // HD
    chunk_factors = jnp.take(factors, head_of, axis=2)
    numerator = jnp.sum(part_sums * chunk_factors, axis=0) + lax.dynamic_slice_in_dim(
        fresh_sums, start, width, 1
    )
    chunk_denominator = jnp.take(denominator, head_of, axis=1)
    attended_part = (numerator / chunk_denominator).astype(jnp.bfloat16)
    attn_mixed = project_out(attended_part, w_o, "seq", 0)
    resid = inputs + attn_mixed
    mixed_in = normalize(resid, moe_gain).astype(jnp.bfloat16)

    expert = me
    chosen = routes.reshape(row_count, TOP)
    gates = route_weights.reshape(row_count, TOP)
    route_scale = jnp.sum(jnp.where(chosen == expert, gates, 0.0), axis=-1)
    gate_up = jnp.dot(mixed_in, expert_in, preferred_element_type=jnp.float32)
    hidden = (jax.nn.silu(gate_up[:, :FFE]) * gate_up[:, FFE:]).astype(jnp.bfloat16)
    produced = jnp.dot(hidden, expert_out, preferred_element_type=jnp.float32)
    own_share = sum_scatter_columns(route_scale[:, None] * produced, "seq")
    share_width = own_share.shape[1]
    resid_share = lax.dynamic_slice_in_dim(resid, me * share_width, share_width, 1)
    return (
        (resid_share + own_share).astype(jnp.bfloat16).reshape(local_requests, NSTEP, share_width)
    )


def solution(mesh):
    in_specs = (
        P("req", None, None),
        P(),
        P(),
        P(None, "seq"),
        P(None, "seq"),
        P("req", "seq", None),
        P("req", "seq", None),
        P("req", "seq"),
        P("req"),
        P("req", None, None),
        P("req", None, None),
        P("seq", "req", None),
        P("seq", None, "req"),
    )
    out_specs = P("req", None, "seq")
    return jax.shard_map(local, mesh=mesh, in_specs=in_specs, out_specs=out_specs, check_vma=False)
```

```python
import math

import jax
import jax.numpy as jnp
from jax import lax
from jax.sharding import PartitionSpec as P

D = 1536
HEADS = 24
KVH = 8
HD = 64
FFE = 512
TOP = 8
NSTEP = 4
PAGE = 16
ATT = 1536
KVD = 512
GROUP = 3
CAP = 12


EPS = 1e-05
NEG = -1e30


def normalize(values, gain):
    power = jnp.mean(values * values, axis=-1, keepdims=True)
    return values * lax.rsqrt(power + EPS) * gain


def rotate(values, position):
    half = values.shape[-1] // 2
    rates = jnp.exp(
        jnp.arange(half, dtype=jnp.float32) * (-2.0 * math.log(10000.0) / values.shape[-1])
    )
    angle = position[..., None, None] * rates
    cosine = jnp.cos(angle)
    sine = jnp.sin(angle)
    first_half = values[..., :half]
    second_half = values[..., half:]
    return jnp.concatenate(
        [first_half * cosine - second_half * sine, second_half * cosine + first_half * sine],
        axis=-1,
    )


def gather_columns(part, axis_name):
    return lax.all_gather(part, axis_name, axis=1, tiled=True)


def sum_scatter_columns(value, axis_name):
    count = lax.axis_size(axis_name)
    rows, width = value.shape
    chunks = jnp.moveaxis(value.reshape(rows, count, width // count), 1, 0)
    pieces = lax.all_to_all(chunks, axis_name, split_axis=0, concat_axis=0, tiled=True)
    return jnp.sum(pieces, axis=0)


def local(
    x_in,
    attn_gain,
    moe_gain,
    w_qkv,
    w_o,
    cache_k,
    cache_v,
    page_map,
    lengths,
    routes,
    route_weights,
    w_gate_up,
    w_down,
):
    expert_in = lax.all_gather(w_gate_up[0], "req", axis=0, tiled=True)
    expert_out = lax.all_gather(w_down[0], "req", axis=1, tiled=True)

    seq_count = lax.axis_size("seq")
    me = lax.axis_index("seq")
    local_requests = x_in.shape[0]
    row_count = local_requests * NSTEP
    inputs = x_in.astype(jnp.float32).reshape(row_count, D)
    normed = normalize(inputs, attn_gain).astype(jnp.bfloat16)
    projected = gather_columns(
        jnp.dot(normed, w_qkv, preferred_element_type=jnp.float32), "seq"
    )
    queries = projected[:, :ATT].reshape(local_requests, NSTEP, HEADS, HD)
    keys_new = projected[:, ATT : ATT + KVD].reshape(local_requests, NSTEP, KVH, HD)
    values_new = (
        projected[:, ATT + KVD :].reshape(local_requests, NSTEP, KVH, HD).astype(jnp.bfloat16)
    )
    position = (lengths[:, None] + jnp.arange(NSTEP, dtype=jnp.int32)[None, :]).astype(jnp.float32)
    queries = (
        rotate(queries, position)
        .astype(jnp.bfloat16)
        .reshape(local_requests, NSTEP, KVH, GROUP, HD)
    )
    keys_new = rotate(keys_new, position).astype(jnp.bfloat16)
    scale = HD ** (-0.5)
    slot_count = cache_k.shape[1]
    cached_keys = cache_k.reshape(local_requests, slot_count, KVH, HD)
    cached_values = cache_v.reshape(local_requests, slot_count, KVH, HD)
    slot_position = (
        page_map[:, :, None] * PAGE + jnp.arange(PAGE, dtype=jnp.int32)[None, None, :]
    ).reshape(local_requests, slot_count)
    live = (slot_position < lengths[:, None])[:, None, None, None, :]
    scores = (
        jnp.einsum("rskgd,rtkd->rskgt", queries, cached_keys, preferred_element_type=jnp.float32)
        * scale
    )
    scores = jnp.where(live, scores, NEG)
    local_top = jnp.max(scores, axis=-1)
    exp_scores = jnp.where(live, jnp.exp(scores - local_top[..., None]), 0.0)
    local_total = jnp.sum(exp_scores, axis=-1).reshape(row_count, HEADS)
    local_sums = jnp.einsum(
        "rskgt,rtkd->rskgd",
        exp_scores.astype(jnp.bfloat16),
        cached_values,
        preferred_element_type=jnp.float32,
    ).reshape(row_count, ATT)
    local_top = local_top.reshape(row_count, HEADS)

    width = ATT // seq_count
    sum_chunks = jnp.moveaxis(local_sums.reshape(row_count, seq_count, width), 1, 0)
    extras = jnp.broadcast_to(
        jnp.concatenate([local_total, local_top], axis=1)[None],
        (seq_count, row_count, 2 * HEADS),
    )
    outgoing = jnp.concatenate([sum_chunks, extras], axis=2)
    arrived = lax.all_to_all(outgoing, "seq", split_axis=0, concat_axis=0, tiled=True)
    part_sums = arrived[:, :, :width]
    part_totals = arrived[:, :, width : width + HEADS]
    part_tops = arrived[:, :, width + HEADS :]

    causal = (
        jnp.arange(NSTEP, dtype=jnp.int32)[:, None] >= jnp.arange(NSTEP, dtype=jnp.int32)[None, :]
    )[None, :, None, None, :]
    fresh = (
        jnp.einsum("rskgd,rukd->rskgu", queries, keys_new, preferred_element_type=jnp.float32)
        * scale
    )
    fresh = jnp.where(causal, fresh, NEG).reshape(row_count, HEADS, NSTEP)
    cache_top = jnp.max(part_tops, axis=0)
    highest = jnp.maximum(cache_top, jnp.max(fresh, axis=-1))
    factors = jnp.exp(part_tops - highest[None])
    fresh_exp = jnp.exp(fresh - highest[:, :, None])
    denominator = jnp.sum(part_totals * factors, axis=0) + jnp.sum(fresh_exp, axis=-1)
    fresh_probs = fresh_exp.reshape(local_requests, NSTEP, KVH, GROUP, NSTEP).astype(jnp.bfloat16)
    fresh_sums = jnp.einsum(
        "rskgu,rukd->rskgd", fresh_probs, values_new, preferred_element_type=jnp.float32
    ).reshape(row_count, ATT)
    start = me * width
    head_of = (start + jnp.arange(width, dtype=jnp.int32)) // HD
    chunk_factors = jnp.take(factors, head_of, axis=2)
    numerator = jnp.sum(part_sums * chunk_factors, axis=0) + lax.dynamic_slice_in_dim(
        fresh_sums, start, width, 1
    )
    chunk_denominator = jnp.take(denominator, head_of, axis=1)
    attended_part = (numerator / chunk_denominator).astype(jnp.bfloat16)
    attended = gather_columns(attended_part, "seq")
    attn_mixed = gather_columns(
        jnp.dot(attended, w_o, preferred_element_type=jnp.float32), "seq"
    )
    resid = inputs + attn_mixed
    mixed_in = normalize(resid, moe_gain).astype(jnp.bfloat16)

    expert = me
    chosen = routes.reshape(row_count, TOP)
    gates = route_weights.reshape(row_count, TOP)
    route_scale = jnp.sum(jnp.where(chosen == expert, gates, 0.0), axis=-1)
    gate_up = jnp.dot(mixed_in, expert_in, preferred_element_type=jnp.float32)
    hidden = (jax.nn.silu(gate_up[:, :FFE]) * gate_up[:, FFE:]).astype(jnp.bfloat16)
    produced = jnp.dot(hidden, expert_out, preferred_element_type=jnp.float32)
    own_share = sum_scatter_columns(route_scale[:, None] * produced, "seq")
    share_width = own_share.shape[1]
    resid_share = lax.dynamic_slice_in_dim(resid, me * share_width, share_width, 1)
    return (
        (resid_share + own_share).astype(jnp.bfloat16).reshape(local_requests, NSTEP, share_width)
    )


def solution(mesh):
    in_specs = (
        P("req", None, None),
        P(),
        P(),
        P(None, "seq"),
        P(None, "seq"),
        P("req", "seq", None),
        P("req", "seq", None),
        P("req", "seq"),
        P("req"),
        P("req", None, None),
        P("req", None, None),
        P("seq", "req", None),
        P("seq", None, "req"),
    )
    out_specs = P("req", None, "seq")
    return jax.shard_map(local, mesh=mesh, in_specs=in_specs, out_specs=out_specs, check_vma=False)
```

```python
import math

import jax
import jax.numpy as jnp
from jax import lax
from jax.sharding import PartitionSpec as P

D = 1536
HEADS = 24
KVH = 8
HD = 64
FFE = 512
TOP = 8
NSTEP = 4
PAGE = 16
ATT = 1536
KVD = 512
GROUP = 3
CAP = 12


EPS = 1e-05
NEG = -1e30


def normalize(values, gain):
    power = jnp.mean(values * values, axis=-1, keepdims=True)
    return values * lax.rsqrt(power + EPS) * gain


def rotate(values, position):
    half = values.shape[-1] // 2
    rates = jnp.exp(
        jnp.arange(half, dtype=jnp.float32) * (-2.0 * math.log(10000.0) / values.shape[-1])
    )
    angle = position[..., None, None] * rates
    cosine = jnp.cos(angle)
    sine = jnp.sin(angle)
    first_half = values[..., :half]
    second_half = values[..., half:]
    return jnp.concatenate(
        [first_half * cosine - second_half * sine, second_half * cosine + first_half * sine],
        axis=-1,
    )


def gather_columns(part, axis_name):
    count = lax.axis_size(axis_name)
    copies = jnp.broadcast_to(part[None], (count,) + part.shape)
    pieces = lax.all_to_all(copies, axis_name, split_axis=0, concat_axis=0, tiled=True)
    rows, width = part.shape
    return jnp.moveaxis(pieces, 0, 1).reshape(rows, count * width)


def sum_scatter_columns(value, axis_name):
    count = lax.axis_size(axis_name)
    rows, width = value.shape
    chunks = jnp.moveaxis(value.reshape(rows, count, width // count), 1, 0)
    pieces = lax.all_to_all(chunks, axis_name, split_axis=0, concat_axis=0, tiled=True)
    return jnp.sum(pieces, axis=0)


def local(
    x_in,
    attn_gain,
    moe_gain,
    w_qkv,
    w_o,
    cache_k,
    cache_v,
    page_map,
    lengths,
    routes,
    route_weights,
    w_gate_up,
    w_down,
):
    expert_both = lax.all_gather(
        jnp.concatenate([w_gate_up[0], w_down[0].T], axis=1), "req", axis=0, tiled=True
    )
    expert_in = expert_both[:, : 2 * FFE]
    expert_out_t = expert_both[:, 2 * FFE :]

    seq_count = lax.axis_size("seq")
    me = lax.axis_index("seq")
    local_requests = x_in.shape[0]
    row_count = local_requests * NSTEP
    inputs = x_in.astype(jnp.float32).reshape(row_count, D)
    normed = normalize(inputs, attn_gain).astype(jnp.bfloat16)
    projected = gather_columns(
        jnp.dot(normed, w_qkv, preferred_element_type=jnp.float32), "seq"
    )
    queries = projected[:, :ATT].reshape(local_requests, NSTEP, HEADS, HD)
    keys_new = projected[:, ATT : ATT + KVD].reshape(local_requests, NSTEP, KVH, HD)
    values_new = (
        projected[:, ATT + KVD :].reshape(local_requests, NSTEP, KVH, HD).astype(jnp.bfloat16)
    )
    position = (lengths[:, None] + jnp.arange(NSTEP, dtype=jnp.int32)[None, :]).astype(jnp.float32)
    queries = (
        rotate(queries, position)
        .astype(jnp.bfloat16)
        .reshape(local_requests, NSTEP, KVH, GROUP, HD)
    )
    keys_new = rotate(keys_new, position).astype(jnp.bfloat16)
    scale = HD ** (-0.5)
    slot_count = cache_k.shape[1]
    cached_keys = cache_k.reshape(local_requests, slot_count, KVH, HD)
    cached_values = cache_v.reshape(local_requests, slot_count, KVH, HD)
    slot_position = (
        page_map[:, :, None] * PAGE + jnp.arange(PAGE, dtype=jnp.int32)[None, None, :]
    ).reshape(local_requests, slot_count)
    live = (slot_position < lengths[:, None])[:, None, None, None, :]
    scores = (
        jnp.einsum("rskgd,rtkd->rskgt", queries, cached_keys, preferred_element_type=jnp.float32)
        * scale
    )
    scores = jnp.where(live, scores, NEG)
    local_top = jnp.max(scores, axis=-1)
    exp_scores = jnp.where(live, jnp.exp(scores - local_top[..., None]), 0.0)
    local_total = jnp.sum(exp_scores, axis=-1).reshape(row_count, HEADS)
    local_sums = jnp.einsum(
        "rskgt,rtkd->rskgd",
        exp_scores.astype(jnp.bfloat16),
        cached_values,
        preferred_element_type=jnp.float32,
    ).reshape(row_count, ATT)
    local_top = local_top.reshape(row_count, HEADS)

    width = ATT // seq_count
    sum_chunks = jnp.moveaxis(local_sums.reshape(row_count, seq_count, width), 1, 0)
    extras = jnp.broadcast_to(
        jnp.concatenate([local_total, local_top], axis=1)[None],
        (seq_count, row_count, 2 * HEADS),
    )
    outgoing = jnp.concatenate([sum_chunks, extras], axis=2)
    arrived = lax.all_to_all(outgoing, "seq", split_axis=0, concat_axis=0, tiled=True)
    part_sums = arrived[:, :, :width]
    part_totals = arrived[:, :, width : width + HEADS]
    part_tops = arrived[:, :, width + HEADS :]

    causal = (
        jnp.arange(NSTEP, dtype=jnp.int32)[:, None] >= jnp.arange(NSTEP, dtype=jnp.int32)[None, :]
    )[None, :, None, None, :]
    fresh = (
        jnp.einsum("rskgd,rukd->rskgu", queries, keys_new, preferred_element_type=jnp.float32)
        * scale
    )
    fresh = jnp.where(causal, fresh, NEG).reshape(row_count, HEADS, NSTEP)
    cache_top = jnp.max(part_tops, axis=0)
    highest = jnp.maximum(cache_top, jnp.max(fresh, axis=-1))
    factors = jnp.exp(part_tops - highest[None])
    fresh_exp = jnp.exp(fresh - highest[:, :, None])
    denominator = jnp.sum(part_totals * factors, axis=0) + jnp.sum(fresh_exp, axis=-1)
    fresh_probs = fresh_exp.reshape(local_requests, NSTEP, KVH, GROUP, NSTEP).astype(jnp.bfloat16)
    fresh_sums = jnp.einsum(
        "rskgu,rukd->rskgd", fresh_probs, values_new, preferred_element_type=jnp.float32
    ).reshape(row_count, ATT)
    start = me * width
    head_of = (start + jnp.arange(width, dtype=jnp.int32)) // HD
    chunk_factors = jnp.take(factors, head_of, axis=2)
    numerator = jnp.sum(part_sums * chunk_factors, axis=0) + lax.dynamic_slice_in_dim(
        fresh_sums, start, width, 1
    )
    chunk_denominator = jnp.take(denominator, head_of, axis=1)
    attended_part = (numerator / chunk_denominator).astype(jnp.bfloat16)
    attended = gather_columns(attended_part, "seq")
    attn_mixed = gather_columns(
        jnp.dot(attended, w_o, preferred_element_type=jnp.float32), "seq"
    )
    resid = inputs + attn_mixed
    mixed_in = normalize(resid, moe_gain).astype(jnp.bfloat16)

    expert = me
    chosen = routes.reshape(row_count, TOP)
    gates = route_weights.reshape(row_count, TOP)
    route_scale = jnp.sum(jnp.where(chosen == expert, gates, 0.0), axis=-1)
    gate_up = jnp.dot(mixed_in, expert_in, preferred_element_type=jnp.float32)
    hidden = (jax.nn.silu(gate_up[:, :FFE]) * gate_up[:, FFE:]).astype(jnp.bfloat16)
    produced = lax.dot_general(
        hidden, expert_out_t, (((1,), (1,)), ((), ())), preferred_element_type=jnp.float32
    )
    own_share = sum_scatter_columns(route_scale[:, None] * produced, "seq")
    share_width = own_share.shape[1]
    resid_share = lax.dynamic_slice_in_dim(resid, me * share_width, share_width, 1)
    return (
        (resid_share + own_share).astype(jnp.bfloat16).reshape(local_requests, NSTEP, share_width)
    )


def solution(mesh):
    in_specs = (
        P("req", None, None),
        P(),
        P(),
        P(None, "seq"),
        P(None, "seq"),
        P("req", "seq", None),
        P("req", "seq", None),
        P("req", "seq"),
        P("req"),
        P("req", None, None),
        P("req", None, None),
        P("seq", "req", None),
        P("seq", None, "req"),
    )
    out_specs = P("req", None, "seq")
    return jax.shard_map(local, mesh=mesh, in_specs=in_specs, out_specs=out_specs, check_vma=False)
```

```python
import math

import jax
import numpy as np
import jax.numpy as jnp
from jax import lax
from jax.sharding import PartitionSpec as P

D = 1536
HEADS = 24
KVH = 8
HD = 64
FFE = 512
TOP = 8
NSTEP = 4
PAGE = 16
ATT = 1536
KVD = 512
GROUP = 3
CAP = 12


EPS = 1e-05
NEG = -1e30


def normalize(values, gain):
    power = jnp.mean(values * values, axis=-1, keepdims=True)
    return values * lax.rsqrt(power + EPS) * gain


def rotate(values, position):
    half = values.shape[-1] // 2
    rates = jnp.exp(
        jnp.arange(half, dtype=jnp.float32) * (-2.0 * math.log(10000.0) / values.shape[-1])
    )
    angle = position[..., None, None] * rates
    cosine = jnp.cos(angle)
    sine = jnp.sin(angle)
    first_half = values[..., :half]
    second_half = values[..., half:]
    return jnp.concatenate(
        [first_half * cosine - second_half * sine, second_half * cosine + first_half * sine],
        axis=-1,
    )


def gather_columns(part, axis_name):
    count = lax.axis_size(axis_name)
    copies = jnp.broadcast_to(part[None], (count,) + part.shape)
    pieces = lax.all_to_all(copies, axis_name, split_axis=0, concat_axis=0, tiled=True)
    rows, width = part.shape
    return jnp.moveaxis(pieces, 0, 1).reshape(rows, count * width)


def sum_scatter_columns(value, axis_name):
    count = lax.axis_size(axis_name)
    rows, width = value.shape
    chunks = jnp.moveaxis(value.reshape(rows, count, width // count), 1, 0)
    pieces = lax.all_to_all(chunks, axis_name, split_axis=0, concat_axis=0, tiled=True)
    return jnp.sum(pieces, axis=0)


def local(
    x_in,
    attn_gain,
    moe_gain,
    w_qkv,
    w_o,
    cache_k,
    cache_v,
    page_map,
    lengths,
    routes,
    route_weights,
    w_gate_up,
    w_down,
):
    expert_both = lax.all_gather(
        jnp.concatenate([w_gate_up[0], w_down[0].T], axis=1), "req", axis=0, tiled=True
    )
    expert_in = expert_both[:, : 2 * FFE]
    expert_out_t = expert_both[:, 2 * FFE :]

    seq_count = lax.axis_size("seq")
    me = lax.axis_index("seq")
    local_requests = x_in.shape[0]
    row_count = local_requests * NSTEP
    inputs = x_in.astype(jnp.float32).reshape(row_count, D)
    normed = normalize(inputs, attn_gain).astype(jnp.bfloat16)
    projected = gather_columns(
        jnp.dot(normed, w_qkv, preferred_element_type=jnp.float32), "seq"
    )
    queries = projected[:, :ATT].reshape(local_requests, NSTEP, HEADS, HD)
    keys_new = projected[:, ATT : ATT + KVD].reshape(local_requests, NSTEP, KVH, HD)
    values_new = (
        projected[:, ATT + KVD :].reshape(local_requests, NSTEP, KVH, HD).astype(jnp.bfloat16)
    )
    position = (lengths[:, None] + jnp.arange(NSTEP, dtype=jnp.int32)[None, :]).astype(jnp.float32)
    queries = (
        rotate(queries, position)
        .astype(jnp.bfloat16)
        .reshape(local_requests, NSTEP, KVH, GROUP, HD)
    )
    keys_new = rotate(keys_new, position).astype(jnp.bfloat16)
    scale = HD ** (-0.5)
    slot_count = cache_k.shape[1]
    cached_keys = cache_k.reshape(local_requests, slot_count, KVH, HD)
    cached_values = cache_v.reshape(local_requests, slot_count, KVH, HD)
    slot_position = (
        page_map[:, :, None] * PAGE + jnp.arange(PAGE, dtype=jnp.int32)[None, None, :]
    ).reshape(local_requests, slot_count)
    live = (slot_position < lengths[:, None])[:, None, None, None, :]
    scores = (
        jnp.einsum("rskgd,rtkd->rskgt", queries, cached_keys, preferred_element_type=jnp.float32)
        * scale
    )
    scores = jnp.where(live, scores, NEG)
    local_top = jnp.max(scores, axis=-1)
    exp_scores = jnp.where(live, jnp.exp(scores - local_top[..., None]), 0.0)
    local_total = jnp.sum(exp_scores, axis=-1).reshape(row_count, HEADS)
    local_sums = jnp.einsum(
        "rskgt,rtkd->rskgd",
        exp_scores.astype(jnp.bfloat16),
        cached_values,
        preferred_element_type=jnp.float32,
    ).reshape(row_count, ATT)
    local_top = local_top.reshape(row_count, HEADS)

    width = ATT // seq_count
    first_head = np.arange(seq_count) * width // HD
    last_head = (np.arange(seq_count) * width + width - 1) // HD
    pair = np.stack([first_head, last_head], axis=1)
    sum_chunks = jnp.moveaxis(local_sums.reshape(row_count, seq_count, width), 1, 0)
    pair_totals = jnp.moveaxis(local_total[:, pair], 1, 0)
    pair_tops = jnp.moveaxis(local_top[:, pair], 1, 0)
    outgoing = jnp.concatenate([sum_chunks, pair_totals, pair_tops], axis=2)
    arrived = lax.all_to_all(outgoing, "seq", split_axis=0, concat_axis=0, tiled=True)
    part_sums = arrived[:, :, :width]
    part_totals = arrived[:, :, width : width + 2]
    part_tops = arrived[:, :, width + 2 :]

    start = me * width
    my_pair = jnp.stack([start // HD, (start + width - 1) // HD])
    causal = (
        jnp.arange(NSTEP, dtype=jnp.int32)[:, None] >= jnp.arange(NSTEP, dtype=jnp.int32)[None, :]
    )[None, :, None, :]
    pair_queries = jnp.take(
        queries.reshape(local_requests, NSTEP, HEADS, HD), my_pair, axis=2
    )
    pair_keys = jnp.take(keys_new, my_pair // GROUP, axis=2)
    pair_values = jnp.take(values_new, my_pair // GROUP, axis=2)
    fresh = (
        jnp.einsum("rspd,rupd->rspu", pair_queries, pair_keys, preferred_element_type=jnp.float32)
        * scale
    )
    fresh = jnp.where(causal, fresh, NEG).reshape(row_count, 2, NSTEP)
    cache_top = jnp.max(part_tops, axis=0)
    highest = jnp.maximum(cache_top, jnp.max(fresh, axis=-1))
    factors = jnp.exp(part_tops - highest[None])
    fresh_exp = jnp.exp(fresh - highest[:, :, None])
    denominator = jnp.sum(part_totals * factors, axis=0) + jnp.sum(fresh_exp, axis=-1)
    fresh_probs = fresh_exp.reshape(local_requests, NSTEP, 2, NSTEP).astype(jnp.bfloat16)
    fresh_sums = jnp.einsum(
        "rspu,rupd->rspd", fresh_probs, pair_values, preferred_element_type=jnp.float32
    ).reshape(row_count, 2 * HD)
    feature = start + jnp.arange(width, dtype=jnp.int32)
    side = feature // HD - my_pair[0]
    chunk_factors = jnp.take(factors, side, axis=2)
    numerator = jnp.sum(part_sums * chunk_factors, axis=0) + jnp.take(
        fresh_sums, side * HD + feature % HD, axis=1
    )
    chunk_denominator = jnp.take(denominator, side, axis=1)
    attended_part = (numerator / chunk_denominator).astype(jnp.bfloat16)
    attended = gather_columns(attended_part, "seq")
    attn_mixed = gather_columns(
        jnp.dot(attended, w_o, preferred_element_type=jnp.float32), "seq"
    )
    resid = inputs + attn_mixed
    mixed_in = normalize(resid, moe_gain).astype(jnp.bfloat16)

    expert = me
    chosen = routes.reshape(row_count, TOP)
    gates = route_weights.reshape(row_count, TOP)
    route_scale = jnp.sum(jnp.where(chosen == expert, gates, 0.0), axis=-1)
    gate_up = jnp.dot(mixed_in, expert_in, preferred_element_type=jnp.float32)
    hidden = (jax.nn.silu(gate_up[:, :FFE]) * gate_up[:, FFE:]).astype(jnp.bfloat16)
    produced = lax.dot_general(
        hidden, expert_out_t, (((1,), (1,)), ((), ())), preferred_element_type=jnp.float32
    )
    own_share = sum_scatter_columns(route_scale[:, None] * produced, "seq")
    share_width = own_share.shape[1]
    resid_share = lax.dynamic_slice_in_dim(resid, me * share_width, share_width, 1)
    return (
        (resid_share + own_share).astype(jnp.bfloat16).reshape(local_requests, NSTEP, share_width)
    )


def solution(mesh):
    in_specs = (
        P("req", None, None),
        P(),
        P(),
        P(None, "seq"),
        P(None, "seq"),
        P("req", "seq", None),
        P("req", "seq", None),
        P("req", "seq"),
        P("req"),
        P("req", None, None),
        P("req", None, None),
        P("seq", "req", None),
        P("seq", None, "req"),
    )
    out_specs = P("req", None, "seq")
    return jax.shard_map(local, mesh=mesh, in_specs=in_specs, out_specs=out_specs, check_vma=False)
```

```python
import math

import jax
import jax.numpy as jnp
from jax import lax
from jax.sharding import PartitionSpec as P

D = 1536
HEADS = 24
KVH = 8
HD = 64
FFE = 512
TOP = 8
NSTEP = 4
PAGE = 16
ATT = 1536
KVD = 512
GROUP = 3
CAP = 12


EPS = 1e-05
NEG = -1e30


def normalize(values, gain):
    power = jnp.mean(values * values, axis=-1, keepdims=True)
    return values * lax.rsqrt(power + EPS) * gain


def rotate(values, position):
    half = values.shape[-1] // 2
    rates = jnp.exp(
        jnp.arange(half, dtype=jnp.float32) * (-2.0 * math.log(10000.0) / values.shape[-1])
    )
    angle = position[..., None, None] * rates
    cosine = jnp.cos(angle)
    sine = jnp.sin(angle)
    first_half = values[..., :half]
    second_half = values[..., half:]
    return jnp.concatenate(
        [first_half * cosine - second_half * sine, second_half * cosine + first_half * sine],
        axis=-1,
    )


def gather_columns(part, axis_name):
    count = lax.axis_size(axis_name)
    copies = jnp.broadcast_to(part[None], (count,) + part.shape)
    pieces = lax.all_to_all(copies, axis_name, split_axis=0, concat_axis=0, tiled=True)
    rows, width = part.shape
    return jnp.moveaxis(pieces, 0, 1).reshape(rows, count * width)


def sum_scatter_columns(value, axis_name):
    count = lax.axis_size(axis_name)
    rows, width = value.shape
    chunks = jnp.moveaxis(value.reshape(rows, count, width // count), 1, 0)
    pieces = lax.all_to_all(chunks, axis_name, split_axis=0, concat_axis=0, tiled=True)
    return jnp.sum(pieces, axis=0)


def local(
    x_in,
    attn_gain,
    moe_gain,
    w_qkv,
    w_o,
    cache_k,
    cache_v,
    page_map,
    lengths,
    routes,
    route_weights,
    w_gate_up,
    w_down,
):
    expert_both = lax.all_gather(
        jnp.concatenate([w_gate_up[0], w_down[0].T], axis=1), "req", axis=0, tiled=True
    )
    expert_in = expert_both[:, : 2 * FFE]
    expert_out_t = expert_both[:, 2 * FFE :]

    seq_count = lax.axis_size("seq")
    me = lax.axis_index("seq")
    local_requests = x_in.shape[0]
    row_count = local_requests * NSTEP
    inputs = x_in.astype(jnp.float32).reshape(row_count, D)
    normed = normalize(inputs, attn_gain).astype(jnp.bfloat16)
    projected = gather_columns(
        jnp.dot(normed, w_qkv, preferred_element_type=jnp.float32), "seq"
    )
    queries = projected[:, :ATT].reshape(local_requests, NSTEP, HEADS, HD)
    keys_new = projected[:, ATT : ATT + KVD].reshape(local_requests, NSTEP, KVH, HD)
    values_new = (
        projected[:, ATT + KVD :].reshape(local_requests, NSTEP, KVH, HD).astype(jnp.bfloat16)
    )
    position = (lengths[:, None] + jnp.arange(NSTEP, dtype=jnp.int32)[None, :]).astype(jnp.float32)
    queries = (
        rotate(queries, position)
        .astype(jnp.bfloat16)
        .reshape(local_requests, NSTEP, KVH, GROUP, HD)
    )
    keys_new = rotate(keys_new, position).astype(jnp.bfloat16)
    scale = HD ** (-0.5)
    slot_count = cache_k.shape[1]
    cached_keys = cache_k.reshape(local_requests, slot_count, KVH, HD)
    cached_values = cache_v.reshape(local_requests, slot_count, KVH, HD)
    slot_position = (
        page_map[:, :, None] * PAGE + jnp.arange(PAGE, dtype=jnp.int32)[None, None, :]
    ).reshape(local_requests, slot_count)
    live = (slot_position < lengths[:, None])[:, None, None, None, :]
    scores = (
        jnp.einsum("rskgd,rtkd->rskgt", queries, cached_keys, preferred_element_type=jnp.float32)
        * scale
    )
    scores = jnp.where(live, scores, NEG)
    local_top = jnp.max(scores, axis=-1)
    exp_scores = jnp.where(live, jnp.exp(scores - local_top[..., None]), 0.0)
    local_total = jnp.sum(exp_scores, axis=-1).reshape(row_count, HEADS)
    local_sums = jnp.einsum(
        "rskgt,rtkd->rskgd",
        exp_scores.astype(jnp.bfloat16),
        cached_values,
        preferred_element_type=jnp.float32,
    ).reshape(row_count, ATT)
    local_top = local_top.reshape(row_count, HEADS)

    width = ATT // seq_count
    pair_starts = [min(c * width // HD, HEADS - 2) for c in range(seq_count)]
    sum_chunks = jnp.moveaxis(local_sums.reshape(row_count, seq_count, width), 1, 0)
    pair_totals = jnp.stack([local_total[:, h : h + 2] for h in pair_starts])
    pair_tops = jnp.stack([local_top[:, h : h + 2] for h in pair_starts])
    outgoing = jnp.concatenate([sum_chunks, pair_totals, pair_tops], axis=2)
    arrived = lax.all_to_all(outgoing, "seq", split_axis=0, concat_axis=0, tiled=True)
    part_sums = arrived[:, :, :width]
    part_totals = arrived[:, :, width : width + 2]
    part_tops = arrived[:, :, width + 2 :]

    causal = (
        jnp.arange(NSTEP, dtype=jnp.int32)[:, None] >= jnp.arange(NSTEP, dtype=jnp.int32)[None, :]
    )[None, :, None, None, :]
    fresh = (
        jnp.einsum("rskgd,rukd->rskgu", queries, keys_new, preferred_element_type=jnp.float32)
        * scale
    )
    fresh = jnp.where(causal, fresh, NEG).reshape(row_count, HEADS, NSTEP)
    start = me * width
    pair_start = jnp.minimum(start // HD, HEADS - 2)
    fresh_top = jnp.max(fresh, axis=-1)
    highest = jnp.maximum(
        jnp.max(part_tops, axis=0), lax.dynamic_slice_in_dim(fresh_top, pair_start, 2, 1)
    )
    factors = jnp.exp(part_tops - highest[None])
    fresh_exp = jnp.exp(
        fresh - lax.dynamic_update_slice_in_dim(fresh_top, highest, pair_start, 1)[:, :, None]
    )
    denominator = jnp.sum(part_totals * factors, axis=0) + lax.dynamic_slice_in_dim(
        jnp.sum(fresh_exp, axis=-1), pair_start, 2, 1
    )
    fresh_probs = fresh_exp.reshape(local_requests, NSTEP, KVH, GROUP, NSTEP).astype(jnp.bfloat16)
    fresh_sums = jnp.einsum(
        "rskgu,rukd->rskgd", fresh_probs, values_new, preferred_element_type=jnp.float32
    ).reshape(row_count, ATT)
    first = (start + jnp.arange(width, dtype=jnp.int32)) // HD == pair_start
    chunk_factors = jnp.where(first[None, None, :], factors[:, :, 0:1], factors[:, :, 1:2])
    numerator = jnp.sum(part_sums * chunk_factors, axis=0) + lax.dynamic_slice_in_dim(
        fresh_sums, start, width, 1
    )
    chunk_denominator = jnp.where(first[None, :], denominator[:, 0:1], denominator[:, 1:2])
    attended_part = (numerator / chunk_denominator).astype(jnp.bfloat16)
    attended = gather_columns(attended_part, "seq")
    attn_mixed = gather_columns(
        jnp.dot(attended, w_o, preferred_element_type=jnp.float32), "seq"
    )
    resid = inputs + attn_mixed
    mixed_in = normalize(resid, moe_gain).astype(jnp.bfloat16)

    expert = me
    chosen = routes.reshape(row_count, TOP)
    gates = route_weights.reshape(row_count, TOP)
    route_scale = jnp.sum(jnp.where(chosen == expert, gates, 0.0), axis=-1)
    gate_up = jnp.dot(mixed_in, expert_in, preferred_element_type=jnp.float32)
    hidden = (jax.nn.silu(gate_up[:, :FFE]) * gate_up[:, FFE:]).astype(jnp.bfloat16)
    produced = lax.dot_general(
        hidden, expert_out_t, (((1,), (1,)), ((), ())), preferred_element_type=jnp.float32
    )
    own_share = sum_scatter_columns(route_scale[:, None] * produced, "seq")
    share_width = own_share.shape[1]
    resid_share = lax.dynamic_slice_in_dim(resid, me * share_width, share_width, 1)
    return (
        (resid_share + own_share).astype(jnp.bfloat16).reshape(local_requests, NSTEP, share_width)
    )


def solution(mesh):
    in_specs = (
        P("req", None, None),
        P(),
        P(),
        P(None, "seq"),
        P(None, "seq"),
        P("req", "seq", None),
        P("req", "seq", None),
        P("req", "seq"),
        P("req"),
        P("req", None, None),
        P("req", None, None),
        P("seq", "req", None),
        P("seq", None, "req"),
    )
    out_specs = P("req", None, "seq")
    return jax.shard_map(local, mesh=mesh, in_specs=in_specs, out_specs=out_specs, check_vma=False)
```

```python
import math

import jax
import jax.numpy as jnp
from jax import lax
from jax.sharding import PartitionSpec as P

D = 1536
HEADS = 24
KVH = 8
HD = 64
FFE = 512
TOP = 8
NSTEP = 4
PAGE = 16
ATT = 1536
KVD = 512
GROUP = 3
CAP = 12


EPS = 1e-05
NEG = -1e30


def normalize(values, gain):
    power = jnp.mean(values * values, axis=-1, keepdims=True)
    return values * lax.rsqrt(power + EPS) * gain


def rotate(values, position):
    half = values.shape[-1] // 2
    rates = jnp.exp(
        jnp.arange(half, dtype=jnp.float32) * (-2.0 * math.log(10000.0) / values.shape[-1])
    )
    angle = position[..., None, None] * rates
    cosine = jnp.cos(angle)
    sine = jnp.sin(angle)
    first_half = values[..., :half]
    second_half = values[..., half:]
    return jnp.concatenate(
        [first_half * cosine - second_half * sine, second_half * cosine + first_half * sine],
        axis=-1,
    )


def gather_columns(part, axis_name):
    count = lax.axis_size(axis_name)
    copies = jnp.broadcast_to(part[None], (count,) + part.shape)
    pieces = lax.all_to_all(copies, axis_name, split_axis=0, concat_axis=0, tiled=True)
    rows, width = part.shape
    return jnp.moveaxis(pieces, 0, 1).reshape(rows, count * width)


def sum_scatter_columns(value, axis_name):
    count = lax.axis_size(axis_name)
    rows, width = value.shape
    chunks = jnp.moveaxis(value.reshape(rows, count, width // count), 1, 0)
    pieces = lax.all_to_all(
        chunks.astype(jnp.bfloat16), axis_name, split_axis=0, concat_axis=0, tiled=True
    )
    return jnp.sum(pieces.astype(jnp.float32), axis=0)


def local(
    x_in,
    attn_gain,
    moe_gain,
    w_qkv,
    w_o,
    cache_k,
    cache_v,
    page_map,
    lengths,
    routes,
    route_weights,
    w_gate_up,
    w_down,
):
    expert_both = lax.all_gather(
        jnp.concatenate([w_gate_up[0], w_down[0].T], axis=1), "req", axis=0, tiled=True
    )
    expert_in = expert_both[:, : 2 * FFE]
    expert_out_t = expert_both[:, 2 * FFE :]

    seq_count = lax.axis_size("seq")
    me = lax.axis_index("seq")
    local_requests = x_in.shape[0]
    row_count = local_requests * NSTEP
    inputs = x_in.astype(jnp.float32).reshape(row_count, D)
    normed = normalize(inputs, attn_gain).astype(jnp.bfloat16)
    projected = gather_columns(
        jnp.dot(normed, w_qkv, preferred_element_type=jnp.float32), "seq"
    )
    queries = projected[:, :ATT].reshape(local_requests, NSTEP, HEADS, HD)
    keys_new = projected[:, ATT : ATT + KVD].reshape(local_requests, NSTEP, KVH, HD)
    values_new = (
        projected[:, ATT + KVD :].reshape(local_requests, NSTEP, KVH, HD).astype(jnp.bfloat16)
    )
    position = (lengths[:, None] + jnp.arange(NSTEP, dtype=jnp.int32)[None, :]).astype(jnp.float32)
    queries = (
        rotate(queries, position)
        .astype(jnp.bfloat16)
        .reshape(local_requests, NSTEP, KVH, GROUP, HD)
    )
    keys_new = rotate(keys_new, position).astype(jnp.bfloat16)
    scale = HD ** (-0.5)
    slot_count = cache_k.shape[1]
    cached_keys = cache_k.reshape(local_requests, slot_count, KVH, HD)
    cached_values = cache_v.reshape(local_requests, slot_count, KVH, HD)
    slot_position = (
        page_map[:, :, None] * PAGE + jnp.arange(PAGE, dtype=jnp.int32)[None, None, :]
    ).reshape(local_requests, slot_count)
    live = (slot_position < lengths[:, None])[:, None, None, None, :]
    scores = (
        jnp.einsum("rskgd,rtkd->rskgt", queries, cached_keys, preferred_element_type=jnp.float32)
        * scale
    )
    scores = jnp.where(live, scores, NEG)
    local_top = jnp.max(scores, axis=-1)
    exp_scores = jnp.where(live, jnp.exp(scores - local_top[..., None]), 0.0)
    local_total = jnp.sum(exp_scores, axis=-1).reshape(row_count, HEADS)
    local_sums = jnp.einsum(
        "rskgt,rtkd->rskgd",
        exp_scores.astype(jnp.bfloat16),
        cached_values,
        preferred_element_type=jnp.float32,
    ).reshape(row_count, ATT)
    local_top = local_top.reshape(row_count, HEADS)

    width = ATT // seq_count
    sum_chunks = jnp.moveaxis(local_sums.reshape(row_count, seq_count, width), 1, 0)
    extras = jnp.broadcast_to(
        jnp.concatenate([local_total, local_top], axis=1)[None],
        (seq_count, row_count, 2 * HEADS),
    )
    outgoing = jnp.concatenate([sum_chunks, extras], axis=2)
    arrived = lax.all_to_all(outgoing, "seq", split_axis=0, concat_axis=0, tiled=True)
    part_sums = arrived[:, :, :width]
    part_totals = arrived[:, :, width : width + HEADS]
    part_tops = arrived[:, :, width + HEADS :]

    causal = (
        jnp.arange(NSTEP, dtype=jnp.int32)[:, None] >= jnp.arange(NSTEP, dtype=jnp.int32)[None, :]
    )[None, :, None, None, :]
    fresh = (
        jnp.einsum("rskgd,rukd->rskgu", queries, keys_new, preferred_element_type=jnp.float32)
        * scale
    )
    fresh = jnp.where(causal, fresh, NEG).reshape(row_count, HEADS, NSTEP)
    cache_top = jnp.max(part_tops, axis=0)
    highest = jnp.maximum(cache_top, jnp.max(fresh, axis=-1))
    factors = jnp.exp(part_tops - highest[None])
    fresh_exp = jnp.exp(fresh - highest[:, :, None])
    denominator = jnp.sum(part_totals * factors, axis=0) + jnp.sum(fresh_exp, axis=-1)
    fresh_probs = fresh_exp.reshape(local_requests, NSTEP, KVH, GROUP, NSTEP).astype(jnp.bfloat16)
    fresh_sums = jnp.einsum(
        "rskgu,rukd->rskgd", fresh_probs, values_new, preferred_element_type=jnp.float32
    ).reshape(row_count, ATT)
    start = me * width
    head_of = (start + jnp.arange(width, dtype=jnp.int32)) // HD
    chunk_factors = jnp.take(factors, head_of, axis=2)
    numerator = jnp.sum(part_sums * chunk_factors, axis=0) + lax.dynamic_slice_in_dim(
        fresh_sums, start, width, 1
    )
    chunk_denominator = jnp.take(denominator, head_of, axis=1)
    attended_part = (numerator / chunk_denominator).astype(jnp.bfloat16)
    attended = gather_columns(attended_part, "seq")
    attn_mixed = gather_columns(
        jnp.dot(attended, w_o, preferred_element_type=jnp.float32), "seq"
    )
    resid = inputs + attn_mixed
    mixed_in = normalize(resid, moe_gain).astype(jnp.bfloat16)

    expert = me
    chosen = routes.reshape(row_count, TOP)
    gates = route_weights.reshape(row_count, TOP)
    route_scale = jnp.sum(jnp.where(chosen == expert, gates, 0.0), axis=-1)
    gate_up = jnp.dot(mixed_in, expert_in, preferred_element_type=jnp.float32)
    hidden = (jax.nn.silu(gate_up[:, :FFE]) * gate_up[:, FFE:]).astype(jnp.bfloat16)
    produced = lax.dot_general(
        hidden, expert_out_t, (((1,), (1,)), ((), ())), preferred_element_type=jnp.float32
    )
    own_share = sum_scatter_columns(route_scale[:, None] * produced, "seq")
    share_width = own_share.shape[1]
    resid_share = lax.dynamic_slice_in_dim(resid, me * share_width, share_width, 1)
    return (
        (resid_share + own_share).astype(jnp.bfloat16).reshape(local_requests, NSTEP, share_width)
    )


def solution(mesh):
    in_specs = (
        P("req", None, None),
        P(),
        P(),
        P(None, "seq"),
        P(None, "seq"),
        P("req", "seq", None),
        P("req", "seq", None),
        P("req", "seq"),
        P("req"),
        P("req", None, None),
        P("req", None, None),
        P("seq", "req", None),
        P("seq", None, "req"),
    )
    out_specs = P("req", None, "seq")
    return jax.shard_map(local, mesh=mesh, in_specs=in_specs, out_specs=out_specs, check_vma=False)
```

```python
import math

import jax
import jax.numpy as jnp
from jax import lax
from jax.sharding import PartitionSpec as P

D = 1536
HEADS = 24
KVH = 8
HD = 64
FFE = 512
TOP = 8
NSTEP = 4
PAGE = 16
ATT = 1536
KVD = 512
GROUP = 3
CAP = 12


EPS = 1e-05
NEG = -1e30


def normalize(values, gain):
    power = jnp.mean(values * values, axis=-1, keepdims=True)
    return values * lax.rsqrt(power + EPS) * gain


def rotate(values, position):
    half = values.shape[-1] // 2
    rates = jnp.exp(
        jnp.arange(half, dtype=jnp.float32) * (-2.0 * math.log(10000.0) / values.shape[-1])
    )
    angle = position[..., None, None] * rates
    cosine = jnp.cos(angle)
    sine = jnp.sin(angle)
    first_half = values[..., :half]
    second_half = values[..., half:]
    return jnp.concatenate(
        [first_half * cosine - second_half * sine, second_half * cosine + first_half * sine],
        axis=-1,
    )


def gather_columns(part, axis_name):
    count = lax.axis_size(axis_name)
    copies = jnp.broadcast_to(part[None], (count,) + part.shape)
    pieces = lax.all_to_all(copies, axis_name, split_axis=0, concat_axis=0, tiled=True)
    rows, width = part.shape
    return jnp.moveaxis(pieces, 0, 1).reshape(rows, count * width)


def sum_scatter_columns(value, axis_name):
    count = lax.axis_size(axis_name)
    rows, width = value.shape
    chunks = jnp.moveaxis(value.reshape(rows, count, width // count), 1, 0)
    pieces = lax.all_to_all(
        chunks.astype(jnp.bfloat16), axis_name, split_axis=0, concat_axis=0, tiled=True
    )
    return jnp.sum(pieces.astype(jnp.float32), axis=0)


def local(
    x_in,
    attn_gain,
    moe_gain,
    w_qkv,
    w_o,
    cache_k,
    cache_v,
    page_map,
    lengths,
    routes,
    route_weights,
    w_gate_up,
    w_down,
):
    expert_both = lax.all_gather(
        jnp.concatenate([w_gate_up[0], w_down[0].T], axis=1), "req", axis=0, tiled=True
    )
    expert_in = expert_both[:, : 2 * FFE]
    expert_out_t = expert_both[:, 2 * FFE :]

    seq_count = lax.axis_size("seq")
    me = lax.axis_index("seq")
    local_requests = x_in.shape[0]
    row_count = local_requests * NSTEP
    inputs = x_in.astype(jnp.float32).reshape(row_count, D)
    normed = normalize(inputs, attn_gain).astype(jnp.bfloat16)
    projected = gather_columns(
        jnp.dot(normed, w_qkv, preferred_element_type=jnp.float32), "seq"
    )
    queries = projected[:, :ATT].reshape(local_requests, NSTEP, HEADS, HD)
    keys_new = projected[:, ATT : ATT + KVD].reshape(local_requests, NSTEP, KVH, HD)
    values_new = (
        projected[:, ATT + KVD :].reshape(local_requests, NSTEP, KVH, HD).astype(jnp.bfloat16)
    )
    position = (lengths[:, None] + jnp.arange(NSTEP, dtype=jnp.int32)[None, :]).astype(jnp.float32)
    queries = (
        rotate(queries, position)
        .astype(jnp.bfloat16)
        .reshape(local_requests, NSTEP, KVH, GROUP, HD)
    )
    keys_new = rotate(keys_new, position).astype(jnp.bfloat16)
    scale = HD ** (-0.5)
    slot_count = cache_k.shape[1]
    cached_keys = cache_k.reshape(local_requests, slot_count, KVH, HD)
    cached_values = cache_v.reshape(local_requests, slot_count, KVH, HD)
    slot_position = (
        page_map[:, :, None] * PAGE + jnp.arange(PAGE, dtype=jnp.int32)[None, None, :]
    ).reshape(local_requests, slot_count)
    live = (slot_position < lengths[:, None])[:, None, None, None, :]
    scores = (
        jnp.einsum("rskgd,rtkd->rskgt", queries, cached_keys, preferred_element_type=jnp.float32)
        * scale
    )
    scores = jnp.where(live, scores, NEG)
    local_top = jnp.max(scores, axis=-1)
    exp_scores = jnp.where(live, jnp.exp(scores - local_top[..., None]), 0.0)
    local_total = jnp.sum(exp_scores, axis=-1).reshape(row_count, HEADS)
    local_sums = jnp.einsum(
        "rskgt,rtkd->rskgd",
        exp_scores.astype(jnp.bfloat16),
        cached_values,
        preferred_element_type=jnp.float32,
    ).reshape(row_count, ATT)
    local_top = local_top.reshape(row_count, HEADS)

    width = ATT // seq_count
    sum_chunks = jnp.moveaxis(local_sums.reshape(row_count, seq_count, width), 1, 0)
    extras = jnp.broadcast_to(
        jnp.concatenate([local_total, local_top], axis=1)[None],
        (seq_count, row_count, 2 * HEADS),
    )
    outgoing = jnp.concatenate([sum_chunks, extras], axis=2)
    arrived = lax.all_to_all(outgoing, "seq", split_axis=0, concat_axis=0, tiled=True)
    part_sums = arrived[:, :, :width]
    part_totals = arrived[:, :, width : width + HEADS]
    part_tops = arrived[:, :, width + HEADS :]

    causal = (
        jnp.arange(NSTEP, dtype=jnp.int32)[:, None] >= jnp.arange(NSTEP, dtype=jnp.int32)[None, :]
    )[None, :, None, None, :]
    fresh = (
        jnp.einsum("rskgd,rukd->rskgu", queries, keys_new, preferred_element_type=jnp.float32)
        * scale
    )
    fresh = jnp.where(causal, fresh, NEG).reshape(row_count, HEADS, NSTEP)
    cache_top = jnp.max(part_tops, axis=0)
    highest = jnp.maximum(cache_top, jnp.max(fresh, axis=-1))
    factors = jnp.exp(part_tops - highest[None])
    fresh_exp = jnp.exp(fresh - highest[:, :, None])
    denominator = jnp.sum(part_totals * factors, axis=0) + jnp.sum(fresh_exp, axis=-1)
    fresh_probs = fresh_exp.reshape(local_requests, NSTEP, KVH, GROUP, NSTEP).astype(jnp.bfloat16)
    fresh_sums = jnp.einsum(
        "rskgu,rukd->rskgd", fresh_probs, values_new, preferred_element_type=jnp.float32
    ).reshape(row_count, ATT)
    start = me * width
    head_of = (start + jnp.arange(width, dtype=jnp.int32)) // HD
    chunk_factors = jnp.take(factors, head_of, axis=2)
    numerator = jnp.sum(part_sums * chunk_factors, axis=0) + lax.dynamic_slice_in_dim(
        fresh_sums, start, width, 1
    )
    chunk_denominator = jnp.take(denominator, head_of, axis=1)
    attended_part = (numerator / chunk_denominator).astype(jnp.bfloat16)
    attended = gather_columns(attended_part, "seq")
    attn_mixed = gather_columns(
        jnp.dot(attended, w_o, preferred_element_type=jnp.float32).astype(jnp.bfloat16), "seq"
    ).astype(jnp.float32)
    resid = inputs + attn_mixed
    mixed_in = normalize(resid, moe_gain).astype(jnp.bfloat16)

    expert = me
    chosen = routes.reshape(row_count, TOP)
    gates = route_weights.reshape(row_count, TOP)
    route_scale = jnp.sum(jnp.where(chosen == expert, gates, 0.0), axis=-1)
    gate_up = jnp.dot(mixed_in, expert_in, preferred_element_type=jnp.float32)
    hidden = (jax.nn.silu(gate_up[:, :FFE]) * gate_up[:, FFE:]).astype(jnp.bfloat16)
    produced = lax.dot_general(
        hidden, expert_out_t, (((1,), (1,)), ((), ())), preferred_element_type=jnp.float32
    )
    own_share = sum_scatter_columns(route_scale[:, None] * produced, "seq")
    share_width = own_share.shape[1]
    resid_share = lax.dynamic_slice_in_dim(resid, me * share_width, share_width, 1)
    return (
        (resid_share + own_share).astype(jnp.bfloat16).reshape(local_requests, NSTEP, share_width)
    )


def solution(mesh):
    in_specs = (
        P("req", None, None),
        P(),
        P(),
        P(None, "seq"),
        P(None, "seq"),
        P("req", "seq", None),
        P("req", "seq", None),
        P("req", "seq"),
        P("req"),
        P("req", None, None),
        P("req", None, None),
        P("seq", "req", None),
        P("seq", None, "req"),
    )
    out_specs = P("req", None, "seq")
    return jax.shard_map(local, mesh=mesh, in_specs=in_specs, out_specs=out_specs, check_vma=False)
```

```python
import math

import jax
import jax.numpy as jnp
from jax import lax
from jax.sharding import PartitionSpec as P

D = 1536
HEADS = 24
KVH = 8
HD = 64
FFE = 512
TOP = 8
NSTEP = 4
PAGE = 16
ATT = 1536
KVD = 512
GROUP = 3
CAP = 12


EPS = 1e-05
NEG = -1e30


def normalize(values, gain):
    power = jnp.mean(values * values, axis=-1, keepdims=True)
    return values * lax.rsqrt(power + EPS) * gain


def rotate(values, position):
    half = values.shape[-1] // 2
    rates = jnp.exp(
        jnp.arange(half, dtype=jnp.float32) * (-2.0 * math.log(10000.0) / values.shape[-1])
    )
    angle = position[..., None, None] * rates
    cosine = jnp.cos(angle)
    sine = jnp.sin(angle)
    first_half = values[..., :half]
    second_half = values[..., half:]
    return jnp.concatenate(
        [first_half * cosine - second_half * sine, second_half * cosine + first_half * sine],
        axis=-1,
    )


def gather_columns(part, axis_name):
    count = lax.axis_size(axis_name)
    copies = jnp.broadcast_to(part[None], (count,) + part.shape)
    pieces = lax.all_to_all(copies, axis_name, split_axis=0, concat_axis=0, tiled=True)
    rows, width = part.shape
    return jnp.moveaxis(pieces, 0, 1).reshape(rows, count * width)


def sum_scatter_columns(value, axis_name):
    count = lax.axis_size(axis_name)
    rows, width = value.shape
    chunks = jnp.moveaxis(value.reshape(rows, count, width // count), 1, 0)
    pieces = lax.all_to_all(
        chunks.astype(jnp.bfloat16), axis_name, split_axis=0, concat_axis=0, tiled=True
    )
    return jnp.sum(pieces.astype(jnp.float32), axis=0)


def local(
    x_in,
    attn_gain,
    moe_gain,
    w_qkv,
    w_o,
    cache_k,
    cache_v,
    page_map,
    lengths,
    routes,
    route_weights,
    w_gate_up,
    w_down,
):
    expert_both = lax.all_gather(
        jnp.concatenate([w_gate_up[0], w_down[0].T], axis=1), "req", axis=0, tiled=True
    )
    expert_in = expert_both[:, : 2 * FFE]
    expert_out_t = expert_both[:, 2 * FFE :]

    seq_count = lax.axis_size("seq")
    me = lax.axis_index("seq")
    local_requests = x_in.shape[0]
    row_count = local_requests * NSTEP
    inputs = x_in.astype(jnp.float32).reshape(row_count, D)
    normed = normalize(inputs, attn_gain).astype(jnp.bfloat16)
    projected = gather_columns(
        jnp.dot(normed, w_qkv, preferred_element_type=jnp.float32), "seq"
    )
    queries = projected[:, :ATT].reshape(local_requests, NSTEP, HEADS, HD)
    keys_new = projected[:, ATT : ATT + KVD].reshape(local_requests, NSTEP, KVH, HD)
    values_new = (
        projected[:, ATT + KVD :].reshape(local_requests, NSTEP, KVH, HD).astype(jnp.bfloat16)
    )
    position = (lengths[:, None] + jnp.arange(NSTEP, dtype=jnp.int32)[None, :]).astype(jnp.float32)
    queries = (
        rotate(queries, position)
        .astype(jnp.bfloat16)
        .reshape(local_requests, NSTEP, KVH, GROUP, HD)
    )
    keys_new = rotate(keys_new, position).astype(jnp.bfloat16)
    scale = HD ** (-0.5)
    slot_count = cache_k.shape[1]
    cached_keys = cache_k.reshape(local_requests, slot_count, KVH, HD)
    cached_values = cache_v.reshape(local_requests, slot_count, KVH, HD)
    slot_position = (
        page_map[:, :, None] * PAGE + jnp.arange(PAGE, dtype=jnp.int32)[None, None, :]
    ).reshape(local_requests, slot_count)
    live = (slot_position < lengths[:, None])[:, None, None, None, :]
    scores = (
        jnp.einsum("rskgd,rtkd->rskgt", queries, cached_keys, preferred_element_type=jnp.float32)
        * scale
    )
    scores = jnp.where(live, scores, NEG)
    local_top = jnp.max(scores, axis=-1)
    exp_scores = jnp.where(live, jnp.exp(scores - local_top[..., None]), 0.0)
    local_total = jnp.sum(exp_scores, axis=-1).reshape(row_count, HEADS)
    local_sums = jnp.einsum(
        "rskgt,rtkd->rskgd",
        exp_scores.astype(jnp.bfloat16),
        cached_values,
        preferred_element_type=jnp.float32,
    ).reshape(row_count, ATT)
    local_top = local_top.reshape(row_count, HEADS)

    width = ATT // seq_count
    pair_starts = [min(c * width // HD, HEADS - 2) for c in range(seq_count)]
    sum_chunks = jnp.moveaxis(local_sums.reshape(row_count, seq_count, width), 1, 0)
    pair_totals = jnp.stack([local_total[:, h : h + 2] for h in pair_starts])
    pair_tops = jnp.stack([local_top[:, h : h + 2] for h in pair_starts])
    outgoing = jnp.concatenate([sum_chunks, pair_totals, pair_tops], axis=2)
    arrived = lax.all_to_all(outgoing, "seq", split_axis=0, concat_axis=0, tiled=True)
    part_sums = arrived[:, :, :width]
    part_totals = arrived[:, :, width : width + 2]
    part_tops = arrived[:, :, width + 2 :]

    causal = (
        jnp.arange(NSTEP, dtype=jnp.int32)[:, None] >= jnp.arange(NSTEP, dtype=jnp.int32)[None, :]
    )[None, :, None, None, :]
    fresh = (
        jnp.einsum("rskgd,rukd->rskgu", queries, keys_new, preferred_element_type=jnp.float32)
        * scale
    )
    fresh = jnp.where(causal, fresh, NEG).reshape(row_count, HEADS, NSTEP)
    start = me * width
    pair_start = jnp.minimum(start // HD, HEADS - 2)
    fresh_top = jnp.max(fresh, axis=-1)
    highest = jnp.maximum(
        jnp.max(part_tops, axis=0), lax.dynamic_slice_in_dim(fresh_top, pair_start, 2, 1)
    )
    factors = jnp.exp(part_tops - highest[None])
    fresh_exp = jnp.exp(
        fresh - lax.dynamic_update_slice_in_dim(fresh_top, highest, pair_start, 1)[:, :, None]
    )
    denominator = jnp.sum(part_totals * factors, axis=0) + lax.dynamic_slice_in_dim(
        jnp.sum(fresh_exp, axis=-1), pair_start, 2, 1
    )
    fresh_probs = fresh_exp.reshape(local_requests, NSTEP, KVH, GROUP, NSTEP).astype(jnp.bfloat16)
    fresh_sums = jnp.einsum(
        "rskgu,rukd->rskgd", fresh_probs, values_new, preferred_element_type=jnp.float32
    ).reshape(row_count, ATT)
    first = (start + jnp.arange(width, dtype=jnp.int32)) // HD == pair_start
    chunk_factors = jnp.where(first[None, None, :], factors[:, :, 0:1], factors[:, :, 1:2])
    numerator = jnp.sum(part_sums * chunk_factors, axis=0) + lax.dynamic_slice_in_dim(
        fresh_sums, start, width, 1
    )
    chunk_denominator = jnp.where(first[None, :], denominator[:, 0:1], denominator[:, 1:2])
    attended_part = (numerator / chunk_denominator).astype(jnp.bfloat16)
    attended = gather_columns(attended_part, "seq")
    attn_mixed = gather_columns(
        jnp.dot(attended, w_o, preferred_element_type=jnp.float32).astype(jnp.bfloat16), "seq"
    ).astype(jnp.float32)
    resid = inputs + attn_mixed
    mixed_in = normalize(resid, moe_gain).astype(jnp.bfloat16)

    expert = me
    chosen = routes.reshape(row_count, TOP)
    gates = route_weights.reshape(row_count, TOP)
    route_scale = jnp.sum(jnp.where(chosen == expert, gates, 0.0), axis=-1)
    gate_up = jnp.dot(mixed_in, expert_in, preferred_element_type=jnp.float32)
    hidden = (jax.nn.silu(gate_up[:, :FFE]) * gate_up[:, FFE:]).astype(jnp.bfloat16)
    produced = lax.dot_general(
        hidden, expert_out_t, (((1,), (1,)), ((), ())), preferred_element_type=jnp.float32
    )
    own_share = sum_scatter_columns(route_scale[:, None] * produced, "seq")
    share_width = own_share.shape[1]
    resid_share = lax.dynamic_slice_in_dim(resid, me * share_width, share_width, 1)
    return (
        (resid_share + own_share).astype(jnp.bfloat16).reshape(local_requests, NSTEP, share_width)
    )


def solution(mesh):
    in_specs = (
        P("req", None, None),
        P(),
        P(),
        P(None, "seq"),
        P(None, "seq"),
        P("req", "seq", None),
        P("req", "seq", None),
        P("req", "seq"),
        P("req"),
        P("req", None, None),
        P("req", None, None),
        P("seq", "req", None),
        P("seq", None, "req"),
    )
    out_specs = P("req", None, "seq")
    return jax.shard_map(local, mesh=mesh, in_specs=in_specs, out_specs=out_specs, check_vma=False)
```

```python
import math

import jax
import jax.numpy as jnp
from jax import lax
from jax.sharding import PartitionSpec as P

D = 1536
HEADS = 24
KVH = 8
HD = 64
FFE = 512
TOP = 8
NSTEP = 4
PAGE = 16
ATT = 1536
KVD = 512
GROUP = 3
CAP = 12


EPS = 1e-05
NEG = -1e30


def normalize(values, gain):
    power = jnp.mean(values * values, axis=-1, keepdims=True)
    return values * lax.rsqrt(power + EPS) * gain


def rotate(values, position):
    half = values.shape[-1] // 2
    rates = jnp.exp(
        jnp.arange(half, dtype=jnp.float32) * (-2.0 * math.log(10000.0) / values.shape[-1])
    )
    angle = position[..., None, None] * rates
    cosine = jnp.cos(angle)
    sine = jnp.sin(angle)
    first_half = values[..., :half]
    second_half = values[..., half:]
    return jnp.concatenate(
        [first_half * cosine - second_half * sine, second_half * cosine + first_half * sine],
        axis=-1,
    )


def gather_columns(part, axis_name):
    count = lax.axis_size(axis_name)
    copies = jnp.broadcast_to(part[None], (count,) + part.shape)
    pieces = lax.all_to_all(copies, axis_name, split_axis=0, concat_axis=0, tiled=True)
    rows, width = part.shape
    return jnp.moveaxis(pieces, 0, 1).reshape(rows, count * width)


def sum_scatter_columns(value, axis_name):
    count = lax.axis_size(axis_name)
    rows, width = value.shape
    chunks = jnp.moveaxis(value.reshape(rows, count, width // count), 1, 0)
    pieces = lax.all_to_all(
        chunks.astype(jnp.bfloat16), axis_name, split_axis=0, concat_axis=0, tiled=True
    )
    return jnp.sum(pieces.astype(jnp.float32), axis=0)


def local(
    x_in,
    attn_gain,
    moe_gain,
    w_qkv,
    w_o,
    cache_k,
    cache_v,
    page_map,
    lengths,
    routes,
    route_weights,
    w_gate_up,
    w_down,
):
    expert_both = lax.all_gather(
        jnp.concatenate([w_gate_up[0], w_down[0].T], axis=1), "req", axis=0, tiled=True
    )
    expert_in = expert_both[:, : 2 * FFE]
    expert_out_t = expert_both[:, 2 * FFE :]

    seq_count = lax.axis_size("seq")
    me = lax.axis_index("seq")
    local_requests = x_in.shape[0]
    row_count = local_requests * NSTEP
    inputs_by_request = x_in.astype(jnp.float32)
    normed = normalize(inputs_by_request, attn_gain).astype(jnp.bfloat16)
    projected = gather_columns(
        jnp.einsum("rsd,dc->rsc", normed, w_qkv, preferred_element_type=jnp.float32).reshape(
            row_count, w_qkv.shape[1]
        ),
        "seq",
    )
    inputs = inputs_by_request.reshape(row_count, D)
    queries = projected[:, :ATT].reshape(local_requests, NSTEP, HEADS, HD)
    keys_new = projected[:, ATT : ATT + KVD].reshape(local_requests, NSTEP, KVH, HD)
    values_new = (
        projected[:, ATT + KVD :].reshape(local_requests, NSTEP, KVH, HD).astype(jnp.bfloat16)
    )
    position = (lengths[:, None] + jnp.arange(NSTEP, dtype=jnp.int32)[None, :]).astype(jnp.float32)
    queries = (
        rotate(queries, position)
        .astype(jnp.bfloat16)
        .reshape(local_requests, NSTEP, KVH, GROUP, HD)
    )
    keys_new = rotate(keys_new, position).astype(jnp.bfloat16)
    scale = HD ** (-0.5)
    slot_count = cache_k.shape[1]
    cached_keys = cache_k.reshape(local_requests, slot_count, KVH, HD)
    cached_values = cache_v.reshape(local_requests, slot_count, KVH, HD)
    slot_position = (
        page_map[:, :, None] * PAGE + jnp.arange(PAGE, dtype=jnp.int32)[None, None, :]
    ).reshape(local_requests, slot_count)
    live = (slot_position < lengths[:, None])[:, None, None, None, :]
    scores = (
        jnp.einsum("rskgd,rtkd->rskgt", queries, cached_keys, preferred_element_type=jnp.float32)
        * scale
    )
    scores = jnp.where(live, scores, NEG)
    local_top = jnp.max(scores, axis=-1)
    exp_scores = jnp.where(live, jnp.exp(scores - local_top[..., None]), 0.0)
    local_total = jnp.sum(exp_scores, axis=-1).reshape(row_count, HEADS)
    local_sums = jnp.einsum(
        "rskgt,rtkd->rskgd",
        exp_scores.astype(jnp.bfloat16),
        cached_values,
        preferred_element_type=jnp.float32,
    ).reshape(row_count, ATT)
    local_top = local_top.reshape(row_count, HEADS)

    width = ATT // seq_count
    sum_chunks = jnp.moveaxis(local_sums.reshape(row_count, seq_count, width), 1, 0)
    extras = jnp.broadcast_to(
        jnp.concatenate([local_total, local_top], axis=1)[None],
        (seq_count, row_count, 2 * HEADS),
    )
    outgoing = jnp.concatenate([sum_chunks, extras], axis=2)
    arrived = lax.all_to_all(outgoing, "seq", split_axis=0, concat_axis=0, tiled=True)
    part_sums = arrived[:, :, :width]
    part_totals = arrived[:, :, width : width + HEADS]
    part_tops = arrived[:, :, width + HEADS :]

    causal = (
        jnp.arange(NSTEP, dtype=jnp.int32)[:, None] >= jnp.arange(NSTEP, dtype=jnp.int32)[None, :]
    )[None, :, None, None, :]
    fresh = (
        jnp.einsum("rskgd,rukd->rskgu", queries, keys_new, preferred_element_type=jnp.float32)
        * scale
    )
    fresh = jnp.where(causal, fresh, NEG).reshape(row_count, HEADS, NSTEP)
    cache_top = jnp.max(part_tops, axis=0)
    highest = jnp.maximum(cache_top, jnp.max(fresh, axis=-1))
    factors = jnp.exp(part_tops - highest[None])
    fresh_exp = jnp.exp(fresh - highest[:, :, None])
    denominator = jnp.sum(part_totals * factors, axis=0) + jnp.sum(fresh_exp, axis=-1)
    fresh_probs = fresh_exp.reshape(local_requests, NSTEP, KVH, GROUP, NSTEP).astype(jnp.bfloat16)
    fresh_sums = jnp.einsum(
        "rskgu,rukd->rskgd", fresh_probs, values_new, preferred_element_type=jnp.float32
    ).reshape(row_count, ATT)
    start = me * width
    head_of = (start + jnp.arange(width, dtype=jnp.int32)) // HD
    chunk_factors = jnp.take(factors, head_of, axis=2)
    numerator = jnp.sum(part_sums * chunk_factors, axis=0) + lax.dynamic_slice_in_dim(
        fresh_sums, start, width, 1
    )
    chunk_denominator = jnp.take(denominator, head_of, axis=1)
    attended_part = (numerator / chunk_denominator).astype(jnp.bfloat16)
    attended = gather_columns(attended_part, "seq")
    attn_mixed = gather_columns(
        jnp.dot(attended, w_o, preferred_element_type=jnp.float32).astype(jnp.bfloat16), "seq"
    ).astype(jnp.float32)
    resid = inputs + attn_mixed
    mixed_in = normalize(resid, moe_gain).astype(jnp.bfloat16)

    expert = me
    chosen = routes.reshape(row_count, TOP)
    gates = route_weights.reshape(row_count, TOP)
    route_scale = jnp.sum(jnp.where(chosen == expert, gates, 0.0), axis=-1)
    gate_up = jnp.dot(mixed_in, expert_in, preferred_element_type=jnp.float32)
    hidden = (jax.nn.silu(gate_up[:, :FFE]) * gate_up[:, FFE:]).astype(jnp.bfloat16)
    produced = lax.dot_general(
        hidden, expert_out_t, (((1,), (1,)), ((), ())), preferred_element_type=jnp.float32
    )
    own_share = sum_scatter_columns(route_scale[:, None] * produced, "seq")
    share_width = own_share.shape[1]
    resid_share = lax.dynamic_slice_in_dim(resid, me * share_width, share_width, 1)
    return (
        (resid_share + own_share).astype(jnp.bfloat16).reshape(local_requests, NSTEP, share_width)
    )


def solution(mesh):
    in_specs = (
        P("req", None, None),
        P(),
        P(),
        P(None, "seq"),
        P(None, "seq"),
        P("req", "seq", None),
        P("req", "seq", None),
        P("req", "seq"),
        P("req"),
        P("req", None, None),
        P("req", None, None),
        P("seq", "req", None),
        P("seq", None, "req"),
    )
    out_specs = P("req", None, "seq")
    return jax.shard_map(local, mesh=mesh, in_specs=in_specs, out_specs=out_specs, check_vma=False)
```

```python
import math

import jax
import jax.numpy as jnp
from jax import lax
from jax.sharding import PartitionSpec as P

D = 1536
HEADS = 24
KVH = 8
HD = 64
FFE = 512
TOP = 8
NSTEP = 4
PAGE = 16
ATT = 1536
KVD = 512
GROUP = 3
CAP = 12


EPS = 1e-05
NEG = -1e30


def normalize(values, gain):
    power = jnp.mean(values * values, axis=-1, keepdims=True)
    return values * lax.rsqrt(power + EPS) * gain


def rotate(values, position):
    half = values.shape[-1] // 2
    rates = jnp.exp(
        jnp.arange(half, dtype=jnp.float32) * (-2.0 * math.log(10000.0) / values.shape[-1])
    )
    angle = position[..., None, None] * rates
    cosine = jnp.cos(angle)
    sine = jnp.sin(angle)
    first_half = values[..., :half]
    second_half = values[..., half:]
    return jnp.concatenate(
        [first_half * cosine - second_half * sine, second_half * cosine + first_half * sine],
        axis=-1,
    )


def gather_columns(part, axis_name):
    count = lax.axis_size(axis_name)
    copies = jnp.broadcast_to(part[None], (count,) + part.shape)
    pieces = lax.all_to_all(copies, axis_name, split_axis=0, concat_axis=0, tiled=True)
    rows, width = part.shape
    return jnp.moveaxis(pieces, 0, 1).reshape(rows, count * width)


def sum_scatter_columns(value, axis_name):
    count = lax.axis_size(axis_name)
    rows, width = value.shape
    chunks = jnp.moveaxis(value.reshape(rows, count, width // count), 1, 0)
    pieces = lax.all_to_all(
        chunks.astype(jnp.bfloat16), axis_name, split_axis=0, concat_axis=0, tiled=True
    )
    return jnp.sum(pieces.astype(jnp.float32), axis=0)


def local(
    x_in,
    attn_gain,
    moe_gain,
    w_qkv,
    w_o,
    cache_k,
    cache_v,
    page_map,
    lengths,
    routes,
    route_weights,
    w_gate_up,
    w_down,
):
    expert_both = lax.all_gather(
        jnp.concatenate([w_gate_up[0], w_down[0].T], axis=1), "req", axis=0, tiled=True
    )
    expert_in = expert_both[:, : 2 * FFE]
    expert_out_t = expert_both[:, 2 * FFE :]

    seq_count = lax.axis_size("seq")
    me = lax.axis_index("seq")
    local_requests = x_in.shape[0]
    row_count = local_requests * NSTEP
    inputs_by_request = x_in.astype(jnp.float32)
    normed = normalize(inputs_by_request, attn_gain).astype(jnp.bfloat16)
    projected = gather_columns(
        jnp.einsum("rsd,dc->rsc", normed, w_qkv, preferred_element_type=jnp.float32).reshape(
            row_count, w_qkv.shape[1]
        ),
        "seq",
    )
    inputs = inputs_by_request.reshape(row_count, D)
    queries = projected[:, :ATT].reshape(local_requests, NSTEP, HEADS, HD)
    keys_new = projected[:, ATT : ATT + KVD].reshape(local_requests, NSTEP, KVH, HD)
    values_new = (
        projected[:, ATT + KVD :].reshape(local_requests, NSTEP, KVH, HD).astype(jnp.bfloat16)
    )
    position = (lengths[:, None] + jnp.arange(NSTEP, dtype=jnp.int32)[None, :]).astype(jnp.float32)
    queries = (
        rotate(queries, position)
        .astype(jnp.bfloat16)
        .reshape(local_requests, NSTEP, KVH, GROUP, HD)
    )
    keys_new = rotate(keys_new, position).astype(jnp.bfloat16)
    scale = HD ** (-0.5)
    slot_count = cache_k.shape[1]
    cached_keys = cache_k.reshape(local_requests, slot_count, KVH, HD)
    cached_values = cache_v.reshape(local_requests, slot_count, KVH, HD)
    slot_position = (
        page_map[:, :, None] * PAGE + jnp.arange(PAGE, dtype=jnp.int32)[None, None, :]
    ).reshape(local_requests, slot_count)
    live = (slot_position < lengths[:, None])[:, None, None, None, :]
    scores = (
        jnp.einsum("rskgd,rtkd->rskgt", queries, cached_keys, preferred_element_type=jnp.float32)
        * scale
    )
    scores = jnp.where(live, scores, NEG)
    local_top = jnp.max(scores, axis=-1)
    exp_scores = jnp.where(live, jnp.exp(scores - local_top[..., None]), 0.0)
    local_total = jnp.sum(exp_scores, axis=-1).reshape(row_count, HEADS)
    local_sums = jnp.einsum(
        "rskgt,rtkd->rskgd",
        exp_scores.astype(jnp.bfloat16),
        cached_values,
        preferred_element_type=jnp.float32,
    ).reshape(row_count, ATT)
    local_top = local_top.reshape(row_count, HEADS)

    width = ATT // seq_count
    sum_chunks = jnp.moveaxis(local_sums.reshape(row_count, seq_count, width), 1, 0)
    extras = jnp.broadcast_to(
        jnp.concatenate([local_total, local_top], axis=1)[None],
        (seq_count, row_count, 2 * HEADS),
    )
    outgoing = jnp.concatenate([sum_chunks, extras], axis=2)
    arrived = lax.all_to_all(outgoing, "seq", split_axis=0, concat_axis=0, tiled=True)
    part_sums = arrived[:, :, :width]
    part_totals = arrived[:, :, width : width + HEADS]
    part_tops = arrived[:, :, width + HEADS :]

    causal = (
        jnp.arange(NSTEP, dtype=jnp.int32)[:, None] >= jnp.arange(NSTEP, dtype=jnp.int32)[None, :]
    )[None, :, None, None, :]
    fresh = (
        jnp.einsum("rskgd,rukd->rskgu", queries, keys_new, preferred_element_type=jnp.float32)
        * scale
    )
    fresh = jnp.where(causal, fresh, NEG).reshape(row_count, HEADS, NSTEP)
    cache_top = jnp.max(part_tops, axis=0)
    highest = jnp.maximum(cache_top, jnp.max(fresh, axis=-1))
    factors = jnp.exp(part_tops - highest[None])
    fresh_exp = jnp.exp(fresh - highest[:, :, None])
    denominator = jnp.sum(part_totals * factors, axis=0) + jnp.sum(fresh_exp, axis=-1)
    fresh_probs = fresh_exp.reshape(local_requests, NSTEP, KVH, GROUP, NSTEP).astype(jnp.bfloat16)
    fresh_sums = jnp.einsum(
        "rskgu,rukd->rskgd", fresh_probs, values_new, preferred_element_type=jnp.float32
    ).reshape(row_count, ATT)
    start = me * width
    pair_start = jnp.minimum(start // HD, HEADS - 2)
    first = (start + jnp.arange(width, dtype=jnp.int32)) // HD == pair_start
    pair_factors = lax.dynamic_slice_in_dim(factors, pair_start, 2, 2)
    chunk_factors = jnp.where(first[None, None, :], pair_factors[:, :, 0:1], pair_factors[:, :, 1:2])
    numerator = jnp.sum(part_sums * chunk_factors, axis=0) + lax.dynamic_slice_in_dim(
        fresh_sums, start, width, 1
    )
    pair_denominator = lax.dynamic_slice_in_dim(denominator, pair_start, 2, 1)
    chunk_denominator = jnp.where(first[None, :], pair_denominator[:, 0:1], pair_denominator[:, 1:2])
    attended_part = (numerator / chunk_denominator).astype(jnp.bfloat16)
    attended = gather_columns(attended_part, "seq")
    attn_mixed = gather_columns(
        jnp.dot(attended, w_o, preferred_element_type=jnp.float32).astype(jnp.bfloat16), "seq"
    ).astype(jnp.float32)
    resid = inputs + attn_mixed
    mixed_in = normalize(resid, moe_gain).astype(jnp.bfloat16)

    expert = me
    chosen = routes.reshape(row_count, TOP)
    gates = route_weights.reshape(row_count, TOP)
    route_scale = jnp.sum(jnp.where(chosen == expert, gates, 0.0), axis=-1)
    gate_up = jnp.dot(mixed_in, expert_in, preferred_element_type=jnp.float32)
    hidden = (jax.nn.silu(gate_up[:, :FFE]) * gate_up[:, FFE:]).astype(jnp.bfloat16)
    produced = lax.dot_general(
        hidden, expert_out_t, (((1,), (1,)), ((), ())), preferred_element_type=jnp.float32
    )
    own_share = sum_scatter_columns(route_scale[:, None] * produced, "seq")
    share_width = own_share.shape[1]
    resid_share = lax.dynamic_slice_in_dim(resid, me * share_width, share_width, 1)
    return (
        (resid_share + own_share).astype(jnp.bfloat16).reshape(local_requests, NSTEP, share_width)
    )


def solution(mesh):
    in_specs = (
        P("req", None, None),
        P(),
        P(),
        P(None, "seq"),
        P(None, "seq"),
        P("req", "seq", None),
        P("req", "seq", None),
        P("req", "seq"),
        P("req"),
        P("req", None, None),
        P("req", None, None),
        P("seq", "req", None),
        P("seq", None, "req"),
    )
    out_specs = P("req", None, "seq")
    return jax.shard_map(local, mesh=mesh, in_specs=in_specs, out_specs=out_specs, check_vma=False)
```

```python
import math

import jax
import jax.numpy as jnp
from jax import lax
from jax.sharding import PartitionSpec as P

D = 1536
HEADS = 24
KVH = 8
HD = 64
FFE = 512
TOP = 8
NSTEP = 4
PAGE = 16
ATT = 1536
KVD = 512
GROUP = 3
CAP = 12


EPS = 1e-05
NEG = -1e30


def normalize(values, gain):
    power = jnp.mean(values * values, axis=-1, keepdims=True)
    return values * lax.rsqrt(power + EPS) * gain


def rotate(values, position):
    half = values.shape[-1] // 2
    rates = jnp.exp(
        jnp.arange(half, dtype=jnp.float32) * (-2.0 * math.log(10000.0) / values.shape[-1])
    )
    angle = position[..., None, None] * rates
    cosine = jnp.cos(angle)
    sine = jnp.sin(angle)
    first_half = values[..., :half]
    second_half = values[..., half:]
    return jnp.concatenate(
        [first_half * cosine - second_half * sine, second_half * cosine + first_half * sine],
        axis=-1,
    )


def gather_columns(part, axis_name):
    count = lax.axis_size(axis_name)
    copies = jnp.broadcast_to(part[None], (count,) + part.shape)
    pieces = lax.all_to_all(copies, axis_name, split_axis=0, concat_axis=0, tiled=True)
    rows, width = part.shape
    return jnp.moveaxis(pieces, 0, 1).reshape(rows, count * width)


def sum_scatter_columns(value, axis_name):
    count = lax.axis_size(axis_name)
    rows, width = value.shape
    chunks = jnp.moveaxis(value.reshape(rows, count, width // count), 1, 0)
    pieces = lax.all_to_all(
        chunks.astype(jnp.bfloat16), axis_name, split_axis=0, concat_axis=0, tiled=True
    )
    return jnp.sum(pieces.astype(jnp.float32), axis=0)


def local(
    x_in,
    attn_gain,
    moe_gain,
    w_qkv,
    w_o,
    cache_k,
    cache_v,
    page_map,
    lengths,
    routes,
    route_weights,
    w_gate_up,
    w_down,
):
    expert_both = lax.all_gather(
        jnp.concatenate([w_gate_up[0], w_down[0].T], axis=1), "req", axis=0, tiled=True
    )
    expert_in = expert_both[:, : 2 * FFE]
    expert_out_t = expert_both[:, 2 * FFE :]

    seq_count = lax.axis_size("seq")
    me = lax.axis_index("seq")
    local_requests = x_in.shape[0]
    row_count = local_requests * NSTEP
    inputs_by_request = x_in.astype(jnp.float32)
    normed = normalize(inputs_by_request, attn_gain).astype(jnp.bfloat16)
    projected = gather_columns(
        jnp.einsum("rsd,dc->rsc", normed, w_qkv, preferred_element_type=jnp.float32).reshape(
            row_count, w_qkv.shape[1]
        ),
        "seq",
    )
    inputs = inputs_by_request.reshape(row_count, D)
    queries = projected[:, :ATT].reshape(local_requests, NSTEP, HEADS, HD)
    keys_new = projected[:, ATT : ATT + KVD].reshape(local_requests, NSTEP, KVH, HD)
    values_new = (
        projected[:, ATT + KVD :].reshape(local_requests, NSTEP, KVH, HD).astype(jnp.bfloat16)
    )
    position = (lengths[:, None] + jnp.arange(NSTEP, dtype=jnp.int32)[None, :]).astype(jnp.float32)
    queries = (
        rotate(queries, position)
        .astype(jnp.bfloat16)
        .reshape(local_requests, NSTEP, KVH, GROUP, HD)
    )
    keys_new = rotate(keys_new, position).astype(jnp.bfloat16)
    scale = HD ** (-0.5)
    slot_count = cache_k.shape[1]
    cached_keys = cache_k.reshape(local_requests, slot_count, KVH, HD)
    cached_values = cache_v.reshape(local_requests, slot_count, KVH, HD)
    slot_position = (
        page_map[:, :, None] * PAGE + jnp.arange(PAGE, dtype=jnp.int32)[None, None, :]
    ).reshape(local_requests, slot_count)
    live = (slot_position < lengths[:, None])[:, None, None, None, :]
    scores = (
        jnp.einsum("rskgd,rtkd->rskgt", queries, cached_keys, preferred_element_type=jnp.float32)
        * scale
    )
    scores = jnp.where(live, scores, NEG)
    local_top = jnp.max(scores, axis=-1)
    exp_scores = jnp.where(live, jnp.exp(scores - local_top[..., None]), 0.0)
    local_total = jnp.sum(exp_scores, axis=-1).reshape(row_count, HEADS)
    local_sums = jnp.einsum(
        "rskgt,rtkd->rskgd",
        exp_scores.astype(jnp.bfloat16),
        cached_values,
        preferred_element_type=jnp.float32,
    ).reshape(row_count, ATT)
    local_top = local_top.reshape(row_count, HEADS)

    width = ATT // seq_count
    sum_chunks = jnp.moveaxis(local_sums.reshape(row_count, seq_count, width), 1, 0)
    extras = jnp.broadcast_to(
        jnp.concatenate([local_total, local_top], axis=1)[None],
        (seq_count, row_count, 2 * HEADS),
    )
    outgoing = jnp.concatenate([sum_chunks, extras], axis=2)
    arrived = lax.all_to_all(outgoing, "seq", split_axis=0, concat_axis=0, tiled=True)
    part_sums = arrived[:, :, :width]
    part_totals = arrived[:, :, width : width + HEADS]
    part_tops = arrived[:, :, width + HEADS :]

    causal = (
        jnp.arange(NSTEP, dtype=jnp.int32)[:, None] >= jnp.arange(NSTEP, dtype=jnp.int32)[None, :]
    )[None, :, None, None, :]
    fresh = (
        jnp.einsum("rskgd,rukd->rskgu", queries, keys_new, preferred_element_type=jnp.float32)
        * scale
    )
    fresh = jnp.where(causal, fresh, NEG).reshape(row_count, HEADS, NSTEP)
    cache_top = jnp.max(part_tops, axis=0)
    highest = jnp.maximum(cache_top, jnp.max(fresh, axis=-1))
    factors = jnp.exp(part_tops - highest[None])
    fresh_exp = jnp.exp(fresh - highest[:, :, None])
    denominator = jnp.sum(part_totals * factors, axis=0) + jnp.sum(fresh_exp, axis=-1)
    fresh_probs = fresh_exp.reshape(local_requests, NSTEP, KVH, GROUP, NSTEP).astype(jnp.bfloat16)
    fresh_sums = jnp.einsum(
        "rskgu,rukd->rskgd", fresh_probs, values_new, preferred_element_type=jnp.float32
    ).reshape(row_count, ATT)
    start = me * width
    pair_start = jnp.minimum(start // HD, HEADS - 2)
    first = (start + jnp.arange(width, dtype=jnp.int32)) // HD == pair_start
    pair_factors = lax.dynamic_slice_in_dim(factors, pair_start, 2, 2)
    chunk_factors = jnp.where(first[None, None, :], pair_factors[:, :, 0:1], pair_factors[:, :, 1:2])
    numerator = jnp.sum(part_sums * chunk_factors, axis=0) + lax.dynamic_slice_in_dim(
        fresh_sums, start, width, 1
    )
    pair_denominator = lax.dynamic_slice_in_dim(denominator, pair_start, 2, 1)
    chunk_denominator = jnp.where(first[None, :], pair_denominator[:, 0:1], pair_denominator[:, 1:2])
    attended_part = (numerator / chunk_denominator).astype(jnp.bfloat16)
    attended_pieces = lax.all_to_all(
        jnp.broadcast_to(attended_part[None], (seq_count,) + attended_part.shape),
        "seq", split_axis=0, concat_axis=0, tiled=True,
    )
    attn_mixed = gather_columns(
        jnp.einsum(
            "ird,idc->rc",
            attended_pieces,
            w_o.reshape(seq_count, width, w_o.shape[1]),
            preferred_element_type=jnp.float32,
        ).astype(jnp.bfloat16),
        "seq",
    ).astype(jnp.float32)
    resid = inputs + attn_mixed
    mixed_in = normalize(resid, moe_gain).astype(jnp.bfloat16)

    expert = me
    chosen = routes.reshape(row_count, TOP)
    gates = route_weights.reshape(row_count, TOP)
    route_scale = jnp.sum(jnp.where(chosen == expert, gates, 0.0), axis=-1)
    gate_up = jnp.dot(mixed_in, expert_in, preferred_element_type=jnp.float32)
    hidden = (jax.nn.silu(gate_up[:, :FFE]) * gate_up[:, FFE:]).astype(jnp.bfloat16)
    produced = lax.dot_general(
        hidden, expert_out_t, (((1,), (1,)), ((), ())), preferred_element_type=jnp.float32
    )
    own_share = sum_scatter_columns(route_scale[:, None] * produced, "seq")
    share_width = own_share.shape[1]
    resid_share = lax.dynamic_slice_in_dim(resid, me * share_width, share_width, 1)
    return (
        (resid_share + own_share).astype(jnp.bfloat16).reshape(local_requests, NSTEP, share_width)
    )


def solution(mesh):
    in_specs = (
        P("req", None, None),
        P(),
        P(),
        P(None, "seq"),
        P(None, "seq"),
        P("req", "seq", None),
        P("req", "seq", None),
        P("req", "seq"),
        P("req"),
        P("req", None, None),
        P("req", None, None),
        P("seq", "req", None),
        P("seq", None, "req"),
    )
    out_specs = P("req", None, "seq")
    return jax.shard_map(local, mesh=mesh, in_specs=in_specs, out_specs=out_specs, check_vma=False)
```
